256 devices in a mesh: row: 64 (over x, z, core), col: 4 (over y).
Axes of the slice: x: 4, y: 4, z: 8, core: 2. Of those that a mesh axis runs over, the one named last changes fastest.
Arguments:
- matrix: float32 [128, 4194304], P('col', 'row'), may hold values from -200 to 200
- row_signs: int32 [4194304], P('row'), may hold values from -1 to 1, as said below
- sample_rows: int32 [2048], replicated, may hold values from 0 to 4194303, as said below
- target: float32 [4194304], P('row'), may hold values from -6 to 6
Outputs:
- gradient: float32 [128], replicated
- residual: float32 [4194304], P('row')
The draws below stay inside these ranges and needn't reach their ends.
Inputs may be any that keep to these rules, and one draw needn't show every extreme that they name: `row_signs`: each entry is -1 or +1. `sample_rows`: indices may repeat; 0 and 4194303 are always among them.
All inputs are finite; a program needn't handle non-finite values.
Results may differ from the reference program's by a relative error of at most 0.0003.
Values sent between devices are 32-bit elements; how exact they have to be, the bound alone decides.
No kernel may reach another device: no remote copies, remote signals or barrier semaphores. Data moves between devices by JAX's collectives and lax.ppermute only.
A program may use at most 128 MiB of HBM per device.

```python
import jax
import jax.numpy as jnp
from jax import lax

COLS = 128
ROW_SHARD_COUNT = 65536
SAMPLES = 2048
ROWS = 4194304
N_ROW = 64


def draw_matrix(key, part):
    base = jnp.clip(jax.random.normal(key, (COLS, ROWS), jnp.float32), -6.0, 6.0)
    scales = jnp.exp(jax.random.uniform(jax.random.fold_in(key, 1), (COLS, 1), jnp.float32, 0.0, jnp.log(10.0)))
    return base * scales


def draw_row_signs(key, part):
    return 2 * jax.random.randint(key, (ROWS,), 0, 2, jnp.int32) - 1


def draw_sample_rows(key, part):
    drawn = jax.random.randint(key, (SAMPLES,), 0, ROWS, jnp.int32)
    return drawn.at[0].set(0).at[1].set(ROWS - 1)


def block_scale(rng, dims, split, least, largest):
    def one(dim, parts):
        steps = jax.random.uniform(jax.random.fold_in(jax.random.fold_in(rng, 6), dim), (parts,), jnp.float32, least / len(split), largest / len(split))
        return jnp.repeat(jnp.exp(steps), dims[dim] // parts).reshape((-1,) + (1,) * (len(dims) - dim - 1))

    gain = one(*split[0])
    for cut in split[1:]:
        gain = gain * one(*cut)
    return gain


def noise(stream_key, dims, deviation, limit, pieces=(), kind=jnp.bfloat16):
    factor_of = block_scale(stream_key, dims, pieces, -0.22, 0.18) if pieces else 1.0
    values = jax.random.normal(stream_key, dims, jnp.float32) * deviation * factor_of
    return jnp.minimum(jnp.maximum(values, -limit), limit).astype(kind)


def setup_inputs(seed: int = 0) -> dict:
    arg_keys = jax.random.split(jax.random.key(seed), 5)
    matrix = draw_matrix(jax.random.fold_in(arg_keys[4], 71), 0)
    row_signs = draw_row_signs(jax.random.fold_in(arg_keys[4], 71), 0)
    sample_rows = draw_sample_rows(jax.random.fold_in(arg_keys[4], 71), 0)
    target = noise(arg_keys[3], (ROWS,), 1.0, 6.0, ((0, 64),), jnp.float32)
    return dict(matrix=matrix, row_signs=row_signs, sample_rows=sample_rows, target=target)


def walsh_transform(order):
    index = jnp.arange(order, dtype=jnp.int32)
    common = jnp.bitwise_and(index[:, None], index[None, :])
    parity = jnp.zeros((order, order), jnp.int32)
    for shift in range(max(order.bit_length() - 1, 1)):
        parity = parity + jnp.bitwise_and(jnp.right_shift(common, shift), 1)
    return (1 - 2 * (parity % 2)).astype(jnp.float32)

def reference(matrix, row_signs, sample_rows, target):
    upper_limit = lax.Precision.HIGHEST
    signed = matrix * row_signs.astype(jnp.float32)[None, :]
    block_list = signed.reshape(COLS, N_ROW, ROW_SHARD_COUNT // 128, 128)
    block_list = jnp.einsum('fhig,gz->fhiz', block_list, walsh_transform(128), precision=upper_limit)
    block_list = jnp.einsum('ztdx,dm->ztmx', block_list, walsh_transform(ROW_SHARD_COUNT // 128), precision=upper_limit)
    block_list = jnp.einsum('vego,el->vlgo', block_list, walsh_transform(N_ROW), precision=upper_limit)
    mixed = block_list.reshape(COLS, ROWS) * (1.0 / jnp.sqrt(jnp.float32(ROWS)))
    sketch = jnp.take(mixed, sample_rows, axis=1)
    cross_product_matrix = jnp.dot(sketch, sketch.T, precision=upper_limit) * (ROWS / SAMPLES)
    lower = jnp.linalg.cholesky(cross_product_matrix)
    normal_rhs = jnp.dot(matrix, target, precision=upper_limit)
    gradient = lax.linalg.triangular_solve(lower, normal_rhs[:, None], left_side=True, lower=True)[:, 0]
    estimate = lax.linalg.triangular_solve(lower, gradient[:, None], left_side=True, lower=True, transpose_a=True)[:, 0]
    fitted = jnp.dot(estimate, matrix, precision=upper_limit)
    return (gradient, target - fitted)
```

```python
import functools

import jax
import jax.numpy as jnp
import numpy as np
from jax import lax
from jax.experimental import pallas as pl
from jax.experimental.pallas import tpu as pltpu
from jax.sharding import PartitionSpec as P

F32 = jnp.float32
BF16 = jnp.bfloat16
LANES = 128


def _hadamard(order):
    i = np.arange(order)
    common = i[:, None] & i[None, :]
    parity = np.zeros_like(common)
    while common.any():
        parity ^= common & 1
        common = common >> 1
    return 1 - 2 * parity


def _nt(a, b):
    return lax.dot_general(a, b, (((1,), (1,)), ((), ())), preferred_element_type=F32)


def _iota(shape, dim):
    return lax.broadcasted_iota(jnp.int32, shape, dim)


def _parity_sign(common):
    parity = jnp.zeros_like(common)
    for shift in range(8):
        parity = parity ^ (lax.shift_right_logical(common, shift) & 1)
    return 1.0 - 2.0 * parity.astype(F32)


def _split(x):
    hi = x.astype(BF16)
    return hi, (x - hi.astype(F32)).astype(BF16)


def _butterfly(parts):
    parts = list(parts)
    step = 1
    while step < len(parts):
        for k in range(len(parts)):
            if not k & step:
                a, b = parts[k], parts[k + step]
                parts[k], parts[k + step] = a + b, a - b
        step *= 2
    return parts


def _sketch_kernel(
    packed, place, m0, m1, m2, m3, signs, target, out, had, table, high, low, mixed, got, rhs
):
    step = pl.program_id(0)
    blocks = (m0, m1, m2, m3)
    cols = m0.shape[0]

    @pl.when(step == 0)
    def _():
        had[...] = _parity_sign(_iota((256, 256), 0) & _iota((256, 256), 1)).astype(BF16)
        k = _iota((8, LANES), 0)
        quarter = _iota((8, LANES), 1) // cols
        table[...] = _parity_sign((k & 3 & quarter) | (k & 4)) * (1.0 / 2048.0)
        rhs[...] = jnp.zeros_like(rhs)

    total = rhs[...]
    for q in range(4):
        row0 = pl.multiple_of(q * 128 + step * 16, 16)
        sign = signs[pl.ds(row0, 16), :].astype(F32)
        goal = target[pl.ds(row0, 16), :]
        for half in range(2):
            parts = []
            for u in range(8):
                t = u * 2 + half
                x = blocks[q][:, t * LANES : (t + 1) * LANES]
                total = total + x * goal[t : t + 1, :]
                parts.append(x * sign[t : t + 1, :])
            for u, y in enumerate(_butterfly(parts)):
                hi, lo = _split(y)
                where = (u, slice(q * cols, (q + 1) * cols), slice(half * LANES, (half + 1) * LANES))
                high[where] = hi
                low[where] = lo
    rhs[...] = total
    for u in range(8):
        mixed[pl.ds(pl.multiple_of(step * 2048 + u * 256, 256), 256), :] = _nt(had[...], high[u]) + _nt(had[...], low[u])

    @pl.when(step == pl.num_programs(0) - 1)
    def _():
        @pl.loop(0, 256, unroll=4)
        def _(r):
            at = [pl.ds(pl.multiple_of(i * 2048 + r * 8, 8), 8) for i in range(8)]
            for rows, y in zip(at, _butterfly([mixed[rows, :] for rows in at])):
                mixed[rows, :] = y

        @pl.loop(0, got.shape[0] // 8, unroll=4)
        def _(b):
            base = pl.multiple_of(b * 8, 8)
            for k in range(8):
                p = packed[base + k]
                row = mixed[pl.ds(lax.shift_right_logical(p, 3), 1), :]
                got[pl.ds(base + k, 1), :] = row * table[pl.ds(p & 7, 1), :]

        pick = (_iota((cols, LANES), 0) == _iota((cols, LANES), 1) % cols).astype(BF16)
        ones = jnp.ones((8, LANES), BF16)
        parts = []
        rest = rhs[...]
        for _i in range(3):
            piece = rest.astype(BF16)
            rest = rest - piece.astype(F32)
            parts.append(_nt(ones, piece))
        b_row = (parts[0] + parts[1]) + parts[2]
        b_row = jnp.concatenate([b_row] * (LANES // cols), axis=1)
        mine = _iota((8, LANES), 1) // cols == place[0]
        b_row = jnp.where(mine, b_row, 0.0)
        b_row = jnp.concatenate([b_row, jnp.zeros_like(b_row)], axis=1)
        for chunk in range(8):
            g = got[chunk * 256 : (chunk + 1) * 256, :]
            hi = g.astype(BF16)
            g = g - hi.astype(F32)
            mid = g.astype(BF16)
            lo = (g - mid.astype(F32)).astype(BF16)
            out[chunk, :cols, :] = _nt(pick, hi) + (_nt(pick, mid) + _nt(pick, lo))
            out[chunk, cols:, :] = b_row


def _sketch(matrix, signs, target, packed, place):
    cols, rows = matrix.shape
    grid_spec = pltpu.PrefetchScalarGridSpec(
        num_scalar_prefetch=2,
        grid=(8,),
        in_specs=[
            pl.BlockSpec((cols, 2048), functools.partial(lambda q, i, *_: (0, q * 8 + i), q))
            for q in range(4)
        ]
        + [pl.BlockSpec((512, LANES), lambda i, *_: (0, 0))] * 2,
        out_specs=pl.BlockSpec((8, cols + 8, 256), lambda i, *_: (0, 0, 0)),
        scratch_shapes=[
            pltpu.VMEM((256, 256), BF16),
            pltpu.VMEM((8, LANES), F32),
            pltpu.VMEM((8, LANES, 256), BF16),
            pltpu.VMEM((8, LANES, 256), BF16),
            pltpu.VMEM((16384, LANES), F32),
            pltpu.VMEM((2048, LANES), F32),
            pltpu.VMEM((cols, LANES), F32),
        ],
    )
    return pl.pallas_call(
        _sketch_kernel,
        grid_spec=grid_spec,
        out_shape=jax.ShapeDtypeStruct((8, cols + 8, 256), F32),
        compiler_params=pltpu.CompilerParams(vmem_limit_bytes=48 << 20),
        name="sketch",
    )(packed, place, matrix, matrix, matrix, matrix, signs.reshape(512, LANES), target.reshape(512, LANES))


def _gram_kernel(place, s0, s1, s2, s3, gram, b_row, whole):
    cols = s0.shape[0] - 8
    for k, s in enumerate((s0, s1, s2, s3)):
        at = lax.rem(place[0] + k, 4) * cols
        whole[pl.ds(pl.multiple_of(at, cols), cols), :] = s[:cols, :]
    s = whole[...]
    hi = s.astype(BF16)
    rest = s - hi.astype(F32)
    mid = rest.astype(BF16)
    lo = (rest - mid.astype(F32)).astype(BF16)
    cross = _nt(hi, mid)
    cross2 = _nt(hi, lo)
    small = (cross2 + cross2.T) + _nt(mid, mid)
    gram[...] = _nt(hi, hi) + ((cross + cross.T) + small)
    b_row[...] = (s0[cols:, :LANES] + s2[cols:, :LANES]) + (s1[cols:, :LANES] + s3[cols:, :LANES])


def _gram(place, pieces):
    smem = pl.BlockSpec(memory_space=pltpu.SMEM)
    vmem = pl.BlockSpec(memory_space=pltpu.VMEM)
    return pl.pallas_call(
        _gram_kernel,
        in_specs=[smem] + [vmem] * 4,
        out_specs=[vmem] * 2,
        out_shape=[jax.ShapeDtypeStruct((128, 128), F32), jax.ShapeDtypeStruct((8, 128), F32)],
        scratch_shapes=[pltpu.VMEM((128, 256), F32)],
        name="gram",
    )(place, *pieces)


def _fit_kernel(place, g0, g1, b_row, matrix, gradient, fitted, held, coef, work, sem):
    cols = matrix.shape[0]
    copy = pltpu.make_async_copy(matrix, held, sem)
    copy.start()
    n = 128
    tiles = n // 8
    a = [(g0[8 * t : 8 * t + 8, :] + g1[8 * t : 8 * t + 8, :]) * 2048.0 for t in range(tiles)]
    lane = _iota((8, n), 1)
    sub = _iota((8, n), 0)
    w = [jnp.where(lane == sub + 8 * t, 1.0, 0.0) for t in range(tiles)]
    a.append(b_row[...])
    w.append(jnp.zeros((8, n), F32))
    pivots = jnp.zeros((1, n), F32)
    for k in range(n):
        t, r = divmod(k, 8)
        row_a = a[t][r : r + 1, :]
        row_w = w[t][r : r + 1, :]
        inv = 1.0 / a[t][r : r + 1, k : k + 1]
        pivots = jnp.where(lane[:1] == k, a[t][r : r + 1, k : k + 1], pivots)
        for i in range(t, tiles + 1):
            factor = a[i][:, k : k + 1] * inv
            if i == t:
                factor = jnp.where(sub[:, :1] > r, factor, 0.0)
            if i < tiles:
                a[i] = a[i] - factor * row_a
            else:
                keep = factor
                a[i] = jnp.where(lane >= k + 1, a[i] - factor * row_a, a[i])
            w[i] = w[i] - factor * row_w
    gradient[...] = a[tiles][:1, :] * lax.rsqrt(pivots)
    est = -w[tiles]
    eye = _iota((n, n), 0) == _iota((n, n), 1)
    column = jnp.sum(jnp.where(eye, est[:1, :], 0.0), axis=1, keepdims=True)
    work[...] = jnp.broadcast_to(column, (n, n))
    coef[...] = work[pl.ds(pl.multiple_of(place[0] * cols, cols), cols), :]
    copy.wait()
    e = [coef[8 * i : 8 * i + 8, :] for i in range(cols // 8)]

    @pl.loop(0, 64, unroll=2)
    def _(b):
        out = []
        for k in range(8):
            at = pl.multiple_of((b * 8 + k) * LANES, LANES)
            acc = None
            for i in range(cols // 8):
                term = held[8 * i : 8 * i + 8, pl.ds(at, LANES)] * e[i]
                acc = term if acc is None else acc + term
            out.append(jnp.sum(acc, axis=0, keepdims=True))
        fitted[pl.ds(pl.multiple_of(b * 8, 8), 8), :] = jnp.concatenate(out, axis=0)


def _fit(place, g0, g1, b_row, matrix):
    cols, rows = matrix.shape
    smem = pl.BlockSpec(memory_space=pltpu.SMEM)
    vmem = pl.BlockSpec(memory_space=pltpu.VMEM)
    return pl.pallas_call(
        _fit_kernel,
        in_specs=[smem] + [vmem] * 3 + [pl.BlockSpec(memory_space=pl.ANY)],
        out_specs=[vmem] * 2,
        out_shape=[jax.ShapeDtypeStruct((1, 128), F32), jax.ShapeDtypeStruct((rows // LANES, LANES), F32)],
        scratch_shapes=[
            pltpu.VMEM((cols, rows), F32),
            pltpu.VMEM((cols, LANES), F32),
            pltpu.VMEM((128, 128), F32),
            pltpu.SemaphoreType.DMA,
        ],
        compiler_params=pltpu.CompilerParams(vmem_limit_bytes=32 << 20),
        name="fit",
    )(place, g0, g1, b_row, matrix)


def _row_pairs(dx=0, dz=None, dcore=0):
    pairs = []
    for i in range(64):
        x, z, core = i >> 4, (i >> 1) & 7, i & 1
        to_z = z if dz is None else dz(z)
        pairs.append((i, (((x + dx) % 4) << 4) | (to_z << 1) | (core ^ dcore)))
    return pairs


def _ring(k):
    return [(i, (i + k) % 4) for i in range(4)]


def _sum4(own, others):
    return (own + others[1]) + (others[0] + others[2])


def body(matrix, row_signs, sample_rows, target):
    cols, rows = matrix.shape
    me = lax.axis_index("row")
    place = lax.axis_index("col").reshape(1)
    x, core = me >> 4, me & 1
    order = sample_rows.reshape(2, 4, 256)
    order = jnp.where(core == 1, order[::-1], order)
    doubled = jnp.concatenate([order, order], axis=1)
    order = lax.dynamic_slice_in_dim(doubled, x, 4, 1).reshape(-1)
    common = (order >> 16) & me
    parity = common
    for shift in (4, 2, 1):
        parity = parity ^ (parity >> shift)
    local = order & (rows - 1)
    packed = ((local & 16383) << 3) | ((parity & 1) << 2) | (local >> 14)

    chunks = _sketch(matrix, row_signs, target, packed, place)
    across = lax.ppermute(chunks[4:], "row", _row_pairs(dcore=1))
    chunks = chunks[:4] + across
    piece = _sum4(chunks[0], [lax.ppermute(chunks[k], "row", _row_pairs(dx=k)) for k in (1, 2, 3)])
    for bit in (1, 2, 4):
        piece = piece + lax.ppermute(piece, "row", _row_pairs(dz=lambda z: z ^ bit))
    pieces = [piece] + [lax.ppermute(piece, "col", _ring(-k)) for k in (1, 2, 3)]
    gram, b_row = _gram(place, pieces)
    gram = gram + lax.ppermute(gram, "row", _row_pairs(dcore=1))
    turned = [lax.ppermute(gram, "row", _row_pairs(dx=k)) for k in (1, 2, 3)]
    gradient, fitted = _fit(place, gram + turned[1], turned[0] + turned[2], b_row, matrix)
    fitted = _sum4(fitted, [lax.ppermute(fitted, "col", _ring(k)) for k in (1, 2, 3)])
    residual = target - fitted.reshape(rows)
    return (gradient.reshape(128), residual)


def solution(mesh):
    return jax.shard_map(
        body,
        mesh=mesh,
        in_specs=(P("col", "row"), P("row"), P(), P("row")),
        out_specs=(P(), P("row")),
        check_vma=False,
    )
```

```python
import jax
import jax.numpy as jnp
from jax import lax
from jax.experimental import pallas as pl
from jax.experimental.pallas import tpu as pltpu
from jax.sharding import PartitionSpec as P

F32 = jnp.float32
BF16 = jnp.bfloat16
LANES = 128


def _nt(a, b):
    return lax.dot_general(a, b, (((1,), (1,)), ((), ())), preferred_element_type=F32)


def _iota(shape, dim):
    return lax.broadcasted_iota(jnp.int32, shape, dim)


def _parity_sign(common, bits):
    parity = jnp.zeros_like(common)
    for shift in range(bits):
        parity = parity ^ (lax.shift_right_logical(common, shift) & 1)
    return 1.0 - 2.0 * parity.astype(F32)


def _split(x):
    hi = x.astype(BF16)
    return hi, (x - hi.astype(F32)).astype(BF16)


def _butterfly(parts):
    parts = list(parts)
    step = 1
    while step < len(parts):
        for k in range(len(parts)):
            if not k & step:
                a, b = parts[k], parts[k + step]
                parts[k], parts[k + step] = a + b, a - b
        step *= 2
    return parts


def _sketch_kernel(
    place, samples, wide, signs, target, matrix, out, had, even, odd, held, sign_v, goal_v, mixed, got, turn, rhs, sems
):
    cols = matrix.shape[0]

    def fetch(i, q):
        at = pl.ds(pl.multiple_of(q * 16384 + i * 2048, 2048), 2048)
        return pltpu.make_async_copy(matrix.at[:, at], held.at[:, at], sems.at[i, q])

    small = [
        pltpu.make_async_copy(signs, sign_v, sems.at[8, 0]),
        pltpu.make_async_copy(target, goal_v, sems.at[8, 1]),
    ]
    for copy in small:
        copy.start()
    for i in range(8):
        for q in range(4):
            fetch(i, q).start()
    h = _parity_sign(_iota((128, 128), 0) & _iota((128, 128), 1), 7).astype(BF16)
    had[...] = jnp.concatenate([h, h], axis=1)
    me = place[0]
    rows = wide[...]
    common = lax.shift_right_logical(rows, 16) & me
    for q in range(4):
        group = lax.shift_right_logical(rows, 14) & q
        parity = _parity_sign(common, 6) * _parity_sign(group, 2)
        turn[q] = parity * (1.0 / 2048.0)
    rhs[...] = jnp.zeros_like(rhs)
    for copy in small:
        copy.wait()

    def spread(i, dest):
        totals = [rhs[c * 16 : c * 16 + 16, :] for c in range(cols // 16)]
        for q in range(4):
            row0 = pl.multiple_of(q * 128 + i * 16, 16)
            sign = sign_v[pl.ds(row0, 16), :].astype(F32)
            goal = goal_v[pl.ds(row0, 16), :]
            for c in range(cols // 16):
                parts = []
                for t in range(16):
                    at = pl.multiple_of(q * 16384 + i * 2048 + t * LANES, LANES)
                    x = held[c * 16 : c * 16 + 16, pl.ds(at, LANES)]
                    totals[c] = totals[c] + x * goal[t : t + 1, :]
                    parts.append(x * sign[t : t + 1, :])
                for t, y in enumerate(_butterfly(parts)):
                    hi, lo = _split(y)
                    at = (t & 1) * LANES + q * cols + c * 16
                    dest[t // 2, at : at + 16, :LANES] = hi
                    dest[t // 2, at : at + 16, LANES:] = lo
        for c in range(cols // 16):
            rhs[c * 16 : c * 16 + 16, :] = totals[c]

    def combine(i, source):
        for p in range(8):
            y = _nt(had[...], source[p])
            at = pl.multiple_of(i * 2048 + p * 256, 256)
            mixed[pl.ds(at, 128), :] = y[:, :LANES]
            mixed[pl.ds(at + 128, 128), :] = y[:, LANES:]

    @pl.loop(0, 4)
    def _(s):
        for k in range(2):
            for q in range(4):
                fetch(s * 2 + k, q).wait()
        combine(jnp.maximum(s * 2 - 1, 0), odd)
        spread(s * 2, even)
        combine(s * 2, even)
        spread(s * 2 + 1, odd)

    combine(7, odd)

    @pl.loop(0, 256, unroll=8)
    def _(r):
        at = [pl.ds(pl.multiple_of(i * 2048 + r * 8, 8), 8) for i in range(8)]
        for where, y in zip(at, _butterfly([mixed[where, :] for where in at])):
            mixed[where, :] = y

    core, x = me & 1, lax.shift_right_logical(me, 1 + 3)
    ones = jnp.ones((8, LANES), BF16)
    parts = []
    rest = rhs[...]
    for _i in range(3):
        piece = rest.astype(BF16)
        rest = rest - piece.astype(F32)
        parts.append(_nt(ones, piece))
    b_row = (parts[0] + parts[1]) + parts[2]
    b_row = jnp.concatenate([b_row] * (LANES // cols), axis=1)
    mine = _iota((8, LANES), 1) // cols == place[1]
    b_row = jnp.where(mine, b_row, 0.0)
    b_row = jnp.concatenate([b_row, jnp.zeros_like(b_row)], axis=1)
    eye = (_iota((LANES, LANES), 0) == _iota((LANES, LANES), 1)).astype(BF16)
    eye = jnp.concatenate([eye, eye], axis=1)

    @pl.loop(0, 8)
    def _(chunk):
        group = (core ^ lax.shift_right_logical(chunk, 2)) * 4 + ((x + chunk) & 3)

        @pl.loop(0, 16)
        def _(b):
            base = group * 256 + b * 16
            dest = pl.multiple_of(b * 16, 16)
            for k in range(16):
                got[pl.ds(dest + k, 1), :] = mixed[pl.ds(samples[base + k] & 16383, 1), :]

        hi, lo = _split(got[...])
        y = _nt(eye, jnp.concatenate([hi, lo], axis=1))
        total = None
        for q in range(4):
            term = y[q * cols : (q + 1) * cols, :] * turn[q, pl.ds(group, 1), :]
            total = term if total is None else total + term
        out[chunk, :cols, :] = total
        out[chunk, cols:, :] = b_row


def _sketch(matrix, signs, target, samples, place):
    cols, rows = matrix.shape
    smem = pl.BlockSpec(memory_space=pltpu.SMEM)
    vmem = pl.BlockSpec(memory_space=pltpu.VMEM)
    hbm = pl.BlockSpec(memory_space=pltpu.HBM)
    return pl.pallas_call(
        _sketch_kernel,
        in_specs=[smem, smem, vmem, hbm, hbm, hbm],
        out_specs=vmem,
        scratch_shapes=[
            pltpu.VMEM((LANES, 256), BF16),
            pltpu.VMEM((8, 256, 256), BF16),
            pltpu.VMEM((8, 256, 256), BF16),
            pltpu.VMEM((cols, rows), F32),
            pltpu.VMEM((512, LANES), jnp.int32),
            pltpu.VMEM((512, LANES), F32),
            pltpu.VMEM((16384, LANES), F32),
            pltpu.VMEM((256, LANES), F32),
            pltpu.VMEM((4, 8, 256), F32),
            pltpu.VMEM((cols, LANES), F32),
            pltpu.SemaphoreType.DMA((9, 4)),
        ],
        out_shape=jax.ShapeDtypeStruct((8, cols + 8, 256), F32),
        compiler_params=pltpu.CompilerParams(vmem_limit_bytes=40 << 20),
        name="sketch",
    )(place, samples, samples.reshape(8, 256), signs.reshape(512, LANES), target.reshape(512, LANES), matrix)


def _gram_kernel(place, s0, s1, s2, s3, gram, b_row, whole):
    cols = s0.shape[0] - 8
    for k, s in enumerate((s0, s1, s2, s3)):
        at = lax.rem(place[1] + k, 4) * cols
        whole[pl.ds(pl.multiple_of(at, cols), cols), :] = s[:cols, :]
    s = whole[...]
    hi = s.astype(BF16)
    rest = s - hi.astype(F32)
    mid = rest.astype(BF16)
    lo = (rest - mid.astype(F32)).astype(BF16)
    cross = _nt(hi, mid)
    cross2 = _nt(hi, lo)
    small = (cross2 + cross2.T) + _nt(mid, mid)
    gram[...] = _nt(hi, hi) + ((cross + cross.T) + small)
    b_row[...] = (s0[cols:, :LANES] + s2[cols:, :LANES]) + (s1[cols:, :LANES] + s3[cols:, :LANES])


def _gram(place, pieces):
    smem = pl.BlockSpec(memory_space=pltpu.SMEM)
    vmem = pl.BlockSpec(memory_space=pltpu.VMEM)
    return pl.pallas_call(
        _gram_kernel,
        in_specs=[smem] + [vmem] * 4,
        out_specs=[vmem] * 2,
        out_shape=[jax.ShapeDtypeStruct((128, 128), F32), jax.ShapeDtypeStruct((8, 128), F32)],
        scratch_shapes=[pltpu.VMEM((128, 256), F32)],
        name="gram",
    )(place, *pieces)


def _fit_kernel(place, g0, g1, b_row, matrix, gradient, fitted, held, coef, work, sem):
    cols = matrix.shape[0]
    copy = pltpu.make_async_copy(matrix, held, sem)
    copy.start()
    n = 128
    tiles = n // 8
    a = [(g0[8 * t : 8 * t + 8, :] + g1[8 * t : 8 * t + 8, :]) * 2048.0 for t in range(tiles)]
    lane = _iota((8, n), 1)
    sub = _iota((8, n), 0)
    w = [jnp.where(lane == sub + 8 * t, 1.0, 0.0) for t in range(tiles)]
    a.append(b_row[...])
    w.append(jnp.zeros((8, n), F32))
    pivots = jnp.zeros((1, n), F32)
    for k in range(n):
        t, r = divmod(k, 8)
        row_a = a[t][r : r + 1, :]
        row_w = w[t][r : r + 1, :]
        inv = 1.0 / a[t][r : r + 1, k : k + 1]
        pivots = jnp.where(lane[:1] == k, a[t][r : r + 1, k : k + 1], pivots)
        for i in range(t, tiles + 1):
            factor = a[i][:, k : k + 1] * inv
            if i == t:
                factor = jnp.where(sub[:, :1] > r, factor, 0.0)
            if i < tiles:
                a[i] = a[i] - factor * row_a
            else:
                keep = factor
                a[i] = jnp.where(lane >= k + 1, a[i] - factor * row_a, a[i])
            w[i] = w[i] - factor * row_w
    gradient[...] = a[tiles][:1, :] * lax.rsqrt(pivots)
    est = -w[tiles]
    eye = _iota((n, n), 0) == _iota((n, n), 1)
    column = jnp.sum(jnp.where(eye, est[:1, :], 0.0), axis=1, keepdims=True)
    work[...] = jnp.broadcast_to(column, (n, n))
    coef[...] = work[pl.ds(pl.multiple_of(place[1] * cols, cols), cols), :]
    copy.wait()
    e = [coef[8 * i : 8 * i + 8, :] for i in range(cols // 8)]

    sub = _iota((8, LANES), 0)

    def fold(u, v, half):
        low = (sub & half) == 0
        other = jnp.where(low, v, u)
        return jnp.where(low, u, v) + pltpu.roll(other, half, 0)

    @pl.loop(0, 64, unroll=2)
    def _(b):
        rows = []
        for k in range(8):
            at = pl.multiple_of((b * 8 + k) * LANES, LANES)
            acc = None
            for i in range(cols // 8):
                term = held[8 * i : 8 * i + 8, pl.ds(at, LANES)] * e[i]
                acc = term if acc is None else acc + term
            rows.append(acc)
        for half in (1, 2, 4):
            rows = [fold(rows[k], rows[k + 1], half) for k in range(0, len(rows), 2)]
        fitted[pl.ds(pl.multiple_of(b * 8, 8), 8), :] = rows[0]


def _fit(place, g0, g1, b_row, matrix):
    cols, rows = matrix.shape
    smem = pl.BlockSpec(memory_space=pltpu.SMEM)
    vmem = pl.BlockSpec(memory_space=pltpu.VMEM)
    return pl.pallas_call(
        _fit_kernel,
        in_specs=[smem] + [vmem] * 3 + [pl.BlockSpec(memory_space=pltpu.HBM)],
        out_specs=[vmem] * 2,
        out_shape=[jax.ShapeDtypeStruct((1, 128), F32), jax.ShapeDtypeStruct((rows // LANES, LANES), F32)],
        scratch_shapes=[
            pltpu.VMEM((cols, rows), F32),
            pltpu.VMEM((cols, LANES), F32),
            pltpu.VMEM((128, 128), F32),
            pltpu.SemaphoreType.DMA,
        ],
        compiler_params=pltpu.CompilerParams(vmem_limit_bytes=32 << 20),
        name="fit",
    )(place, g0, g1, b_row, matrix)


def _row_pairs(dx=0, dz=0, dcore=0):
    pairs = []
    for i in range(64):
        x, z, core = i >> 4, (i >> 1) & 7, i & 1
        pairs.append((i, (((x + dx) % 4) << 4) | (((z + dz) % 8) << 1) | (core ^ dcore)))
    return pairs


def _ring(k):
    return [(i, (i + k) % 4) for i in range(4)]


def _sum4(own, others):
    return (own + others[1]) + (others[0] + others[2])


def body(matrix, row_signs, sample_rows, target):
    cols, rows = matrix.shape
    place = jnp.stack([lax.axis_index("row"), lax.axis_index("col")])
    chunks = _sketch(matrix, row_signs, target, sample_rows, place)
    across = lax.ppermute(chunks[4:], "row", _row_pairs(dcore=1))
    chunks = chunks[:4] + across
    piece = _sum4(chunks[0], [lax.ppermute(chunks[k], "row", _row_pairs(dx=k)) for k in (1, 2, 3)])
    piece = piece + lax.ppermute(piece, "row", _row_pairs(dz=4))
    piece = _sum4(piece, [lax.ppermute(piece, "row", _row_pairs(dz=k)) for k in (1, 2, -1)])
    pieces = [piece] + [lax.ppermute(piece, "col", _ring(-k)) for k in (1, 2, 3)]
    gram, b_row = _gram(place, pieces)
    gram = gram + lax.ppermute(gram, "row", _row_pairs(dcore=1))
    turned = [lax.ppermute(gram, "row", _row_pairs(dx=k)) for k in (1, 2, 3)]
    gradient, fitted = _fit(place, gram + turned[1], turned[0] + turned[2], b_row, matrix)
    fitted = _sum4(fitted, [lax.ppermute(fitted, "col", _ring(k)) for k in (1, 2, 3)])
    residual = target - fitted.reshape(rows)
    return (gradient.reshape(128), residual)


def solution(mesh):
    return jax.shard_map(
        body,
        mesh=mesh,
        in_specs=(P("col", "row"), P("row"), P(), P("row")),
        out_specs=(P(), P("row")),
        check_vma=False,
    )
```

```python
import jax
import jax.numpy as jnp
from jax import lax
from jax.experimental import pallas as pl
from jax.experimental.pallas import tpu as pltpu
from jax.sharding import PartitionSpec as P

F32 = jnp.float32
BF16 = jnp.bfloat16
LANES = 128


def _nt(a, b):
    return lax.dot_general(a, b, (((1,), (1,)), ((), ())), preferred_element_type=F32)


def _iota(shape, dim):
    return lax.broadcasted_iota(jnp.int32, shape, dim)


def _parity_sign(common, bits):
    parity = jnp.zeros_like(common)
    for shift in range(bits):
        parity = parity ^ (lax.shift_right_logical(common, shift) & 1)
    return 1.0 - 2.0 * parity.astype(F32)


def _split(x):
    hi = x.astype(BF16)
    return hi, (x - hi.astype(F32)).astype(BF16)


def _butterfly(parts):
    parts = list(parts)
    step = 1
    while step < len(parts):
        for k in range(len(parts)):
            if not k & step:
                a, b = parts[k], parts[k + step]
                parts[k], parts[k + step] = a + b, a - b
        step *= 2
    return parts


def _sketch_kernel(
    samples, signs, target, matrix, out, had, even, odd, held, sign_v, goal_v, mixed, got, turn, rhs, wide, spot, index, sems
):
    cols = matrix.shape[0]

    def fetch(i, q):
        at = pl.ds(pl.multiple_of(q * 16384 + i * 2048, 2048), 2048)
        return pltpu.make_async_copy(matrix.at[:, at], held.at[:, at], sems.at[i, q])

    first = pltpu.make_async_copy(samples, wide, sems.at[8, 2])
    first.start()
    small = [
        pltpu.make_async_copy(signs, sign_v, sems.at[8, 0]),
        pltpu.make_async_copy(target, goal_v, sems.at[8, 1]),
    ]
    for copy in small:
        copy.start()
    for i in range(8):
        for q in range(4):
            fetch(i, q).start()
    h = _parity_sign(_iota((128, 128), 0) & _iota((128, 128), 1), 7).astype(BF16)
    had[...] = jnp.concatenate([h, h], axis=1)
    me = lax.axis_index("row")
    first.wait()
    rows = wide[...]
    spot[...] = rows & 16383
    last = pltpu.make_async_copy(spot, index, sems.at[8, 3])
    last.start()
    common = lax.shift_right_logical(rows, 16) & me
    for q in range(4):
        group = lax.shift_right_logical(rows, 14) & q
        parity = _parity_sign(common, 6) * _parity_sign(group, 2)
        turn[q] = parity * (1.0 / 2048.0)
    rhs[...] = jnp.zeros_like(rhs)
    for copy in small:
        copy.wait()

    def spread(i, dest):
        totals = [rhs[c * 16 : c * 16 + 16, :] for c in range(cols // 16)]
        for q in range(4):
            row0 = pl.multiple_of(q * 128 + i * 16, 16)
            sign = sign_v[pl.ds(row0, 16), :].astype(F32)
            goal = goal_v[pl.ds(row0, 16), :]
            for c in range(cols // 16):
                parts = []
                for t in range(16):
                    at = pl.multiple_of(q * 16384 + i * 2048 + t * LANES, LANES)
                    x = held[c * 16 : c * 16 + 16, pl.ds(at, LANES)]
                    totals[c] = totals[c] + x * goal[t : t + 1, :]
                    parts.append(x * sign[t : t + 1, :])
                for t, y in enumerate(_butterfly(parts)):
                    hi, lo = _split(y)
                    at = (t & 1) * LANES + q * cols + c * 16
                    dest[t // 2, at : at + 16, :LANES] = hi
                    dest[t // 2, at : at + 16, LANES:] = lo
        for c in range(cols // 16):
            rhs[c * 16 : c * 16 + 16, :] = totals[c]

    def combine(i, source):
        for p in range(8):
            y = _nt(had[...], source[p])
            at = pl.multiple_of(i * 2048 + p * 256, 256)
            mixed[pl.ds(at, 128), :] = y[:, :LANES]
            mixed[pl.ds(at + 128, 128), :] = y[:, LANES:]

    @pl.loop(0, 4)
    def _(s):
        for k in range(2):
            for q in range(4):
                fetch(s * 2 + k, q).wait()
        combine(jnp.maximum(s * 2 - 1, 0), odd)
        spread(s * 2, even)
        combine(s * 2, even)
        spread(s * 2 + 1, odd)

    combine(7, odd)

    @pl.loop(0, 256, unroll=8)
    def _(r):
        at = [pl.ds(pl.multiple_of(i * 2048 + r * 8, 8), 8) for i in range(8)]
        for where, y in zip(at, _butterfly([mixed[where, :] for where in at])):
            mixed[where, :] = y

    core, x = me & 1, lax.shift_right_logical(me, 1 + 3)
    ones = jnp.ones((8, LANES), BF16)
    parts = []
    rest = rhs[...]
    for _i in range(3):
        piece = rest.astype(BF16)
        rest = rest - piece.astype(F32)
        parts.append(_nt(ones, piece))
    b_row = (parts[0] + parts[1]) + parts[2]
    b_row = jnp.concatenate([b_row] * (LANES // cols), axis=1)
    mine = _iota((8, LANES), 1) // cols == lax.axis_index("col")
    b_row = jnp.where(mine, b_row, 0.0)
    b_row = jnp.concatenate([b_row, jnp.zeros_like(b_row)], axis=1)
    eye = (_iota((LANES, LANES), 0) == _iota((LANES, LANES), 1)).astype(BF16)
    eye = jnp.concatenate([eye, eye], axis=1)

    last.wait()

    @pl.loop(0, 8)
    def _(chunk):
        group = (core ^ lax.shift_right_logical(chunk, 2)) * 4 + ((x + chunk) & 3)

        @pl.loop(0, 16)
        def _(b):
            line, base = group * 2 + lax.shift_right_logical(b, 3), (b & 7) * 16
            dest = pl.multiple_of(b * 16, 16)
            for k in range(16):
                got[pl.ds(dest + k, 1), :] = mixed[pl.ds(index[line, base + k], 1), :]

        hi, lo = _split(got[...])
        y = _nt(eye, jnp.concatenate([hi, lo], axis=1))
        total = None
        for q in range(4):
            sign = jnp.concatenate([turn[q, pl.ds(group * 2 + k, 1), :] for k in range(2)], axis=1)
            term = y[q * cols : (q + 1) * cols, :] * sign
            total = term if total is None else total + term
        out[chunk, :cols, :] = total
        out[chunk, cols:, :] = b_row


def _sketch(matrix, signs, target, samples):
    cols, rows = matrix.shape
    vmem = pl.BlockSpec(memory_space=pltpu.VMEM)
    hbm = pl.BlockSpec(memory_space=pltpu.HBM)
    return pl.pallas_call(
        _sketch_kernel,
        in_specs=[hbm] * 4,
        out_specs=vmem,
        scratch_shapes=[
            pltpu.VMEM((LANES, 256), BF16),
            pltpu.VMEM((8, 256, 256), BF16),
            pltpu.VMEM((8, 256, 256), BF16),
            pltpu.VMEM((cols, rows), F32),
            pltpu.VMEM((512, LANES), jnp.int32),
            pltpu.VMEM((512, LANES), F32),
            pltpu.VMEM((16384, LANES), F32),
            pltpu.VMEM((256, LANES), F32),
            pltpu.VMEM((4, 16, LANES), F32),
            pltpu.VMEM((cols, LANES), F32),
            pltpu.VMEM((16, LANES), jnp.int32),
            pltpu.VMEM((16, LANES), jnp.int32),
            pltpu.SMEM((16, LANES), jnp.int32),
            pltpu.SemaphoreType.DMA((9, 4)),
        ],
        out_shape=jax.ShapeDtypeStruct((8, cols + 8, 256), F32),
        compiler_params=pltpu.CompilerParams(vmem_limit_bytes=67043328 - (400 << 10)),
        name="sketch",
    )(samples.reshape(16, LANES), signs.reshape(512, LANES), target.reshape(512, LANES), matrix)


def _gram_kernel(s0, s1, s2, s3, gram, b_row, whole):
    cols = s0.shape[0] - 8
    for k, s in enumerate((s0, s1, s2, s3)):
        at = lax.rem(lax.axis_index("col") + k, 4) * cols
        whole[pl.ds(pl.multiple_of(at, cols), cols), :] = s[:cols, :]
    s = whole[...]
    hi = s.astype(BF16)
    rest = s - hi.astype(F32)
    mid = rest.astype(BF16)
    lo = (rest - mid.astype(F32)).astype(BF16)
    cross = _nt(hi, mid)
    cross2 = _nt(hi, lo)
    small = (cross2 + cross2.T) + _nt(mid, mid)
    gram[...] = _nt(hi, hi) + ((cross + cross.T) + small)
    b_row[...] = (s0[cols:, :LANES] + s2[cols:, :LANES]) + (s1[cols:, :LANES] + s3[cols:, :LANES])


def _gram(pieces):
    vmem = pl.BlockSpec(memory_space=pltpu.VMEM)
    return pl.pallas_call(
        _gram_kernel,
        in_specs=[vmem] * 4,
        out_specs=[vmem] * 2,
        out_shape=[jax.ShapeDtypeStruct((128, 128), F32), jax.ShapeDtypeStruct((8, 128), F32)],
        scratch_shapes=[pltpu.VMEM((128, 256), F32)],
        compiler_params=pltpu.CompilerParams(vmem_limit_bytes=8 << 20),
        name="gram",
    )(*pieces)


def _fit_kernel(g0, g1, b_row, matrix, gradient, fitted, held, coef, work, sem):
    cols = matrix.shape[0]
    copy = pltpu.make_async_copy(matrix, held, sem)
    copy.start()
    n = 128
    tiles = n // 8
    a = [(g0[8 * t : 8 * t + 8, :] + g1[8 * t : 8 * t + 8, :]) * 2048.0 for t in range(tiles)]
    lane = _iota((8, n), 1)
    sub = _iota((8, n), 0)
    w = [jnp.where(lane == sub + 8 * t, 1.0, 0.0) for t in range(tiles)]
    a.append(b_row[...])
    w.append(jnp.zeros((8, n), F32))
    pivots = jnp.zeros((1, n), F32)
    for k in range(n):
        t, r = divmod(k, 8)
        row_a = a[t][r : r + 1, :]
        row_w = w[t][r : r + 1, :]
        inv = 1.0 / a[t][r : r + 1, k : k + 1]
        pivots = jnp.where(lane[:1] == k, a[t][r : r + 1, k : k + 1], pivots)
        for i in range(t, tiles + 1):
            factor = a[i][:, k : k + 1] * inv
            if i == t:
                factor = jnp.where(sub[:, :1] > r, factor, 0.0)
            if i < tiles:
                a[i] = a[i] - factor * row_a
            else:
                keep = factor
                a[i] = jnp.where(lane >= k + 1, a[i] - factor * row_a, a[i])
            w[i] = w[i] - factor * row_w
    gradient[...] = a[tiles][:1, :] * lax.rsqrt(pivots)
    est = -w[tiles]
    eye = _iota((n, n), 0) == _iota((n, n), 1)
    column = jnp.sum(jnp.where(eye, est[:1, :], 0.0), axis=1, keepdims=True)
    work[...] = jnp.broadcast_to(column, (n, n))
    coef[...] = work[pl.ds(pl.multiple_of(lax.axis_index("col") * cols, cols), cols), :]
    copy.wait()
    e = [coef[8 * i : 8 * i + 8, :] for i in range(cols // 8)]

    sub = _iota((8, LANES), 0)

    def fold(u, v, half):
        low = (sub & half) == 0
        other = jnp.where(low, v, u)
        return jnp.where(low, u, v) + pltpu.roll(other, half, 0)

    @pl.loop(0, 64, unroll=2)
    def _(b):
        rows = []
        for k in range(8):
            at = pl.multiple_of((b * 8 + k) * LANES, LANES)
            acc = None
            for i in range(cols // 8):
                term = held[8 * i : 8 * i + 8, pl.ds(at, LANES)] * e[i]
                acc = term if acc is None else acc + term
            rows.append(acc)
        for half in (1, 2, 4):
            rows = [fold(rows[k], rows[k + 1], half) for k in range(0, len(rows), 2)]
        fitted[pl.ds(pl.multiple_of(b * 8, 8), 8), :] = rows[0]


def _fit(g0, g1, b_row, matrix):
    cols, rows = matrix.shape
    vmem = pl.BlockSpec(memory_space=pltpu.VMEM)
    return pl.pallas_call(
        _fit_kernel,
        in_specs=[vmem] * 3 + [pl.BlockSpec(memory_space=pltpu.HBM)],
        out_specs=[vmem] * 2,
        out_shape=[jax.ShapeDtypeStruct((1, 128), F32), jax.ShapeDtypeStruct((rows // LANES, LANES), F32)],
        scratch_shapes=[
            pltpu.VMEM((cols, rows), F32),
            pltpu.VMEM((cols, LANES), F32),
            pltpu.VMEM((128, 128), F32),
            pltpu.SemaphoreType.DMA,
        ],
        compiler_params=pltpu.CompilerParams(vmem_limit_bytes=67043328 - (1 << 20)),
        name="fit",
    )(g0, g1, b_row, matrix)


def _row_pairs(dx=0, dz=0, dcore=0):
    pairs = []
    for i in range(64):
        x, z, core = i >> 4, (i >> 1) & 7, i & 1
        pairs.append((i, (((x + dx) % 4) << 4) | (((z + dz) % 8) << 1) | (core ^ dcore)))
    return pairs


def _ring(k):
    return [(i, (i + k) % 4) for i in range(4)]


def _sum4(own, others):
    return (own + others[1]) + (others[0] + others[2])


def body(matrix, row_signs, sample_rows, target):
    cols, rows = matrix.shape
    chunks = _sketch(matrix, row_signs, target, sample_rows)
    across = lax.ppermute(chunks[4:], "row", _row_pairs(dcore=1))
    chunks = chunks[:4] + across
    piece = _sum4(chunks[0], [lax.ppermute(chunks[k], "row", _row_pairs(dx=k)) for k in (1, 2, 3)])
    piece = piece + lax.ppermute(piece, "row", _row_pairs(dz=4))
    piece = _sum4(piece, [lax.ppermute(piece, "row", _row_pairs(dz=k)) for k in (1, 2, -1)])
    pieces = [piece] + [lax.ppermute(piece, "col", _ring(-k)) for k in (1, 2, 3)]
    gram, b_row = _gram(pieces)
    gram = gram + lax.ppermute(gram, "row", _row_pairs(dcore=1))
    turned = [lax.ppermute(gram, "row", _row_pairs(dx=k)) for k in (1, 2, 3)]
    gradient, fitted = _fit(gram + turned[1], turned[0] + turned[2], b_row, matrix)
    fitted = _sum4(fitted, [lax.ppermute(fitted, "col", _ring(k)) for k in (1, 2, 3)])
    residual = target - fitted.reshape(rows)
    return (gradient.reshape(128), residual)


def solution(mesh):
    return jax.shard_map(
        body,
        mesh=mesh,
        in_specs=(P("col", "row"), P("row"), P(), P("row")),
        out_specs=(P(), P("row")),
        check_vma=False,
    )
```

```python
import jax
import jax.numpy as jnp
from jax import lax
from jax.experimental import pallas as pl
from jax.experimental.pallas import tpu as pltpu
from jax.sharding import PartitionSpec as P

F32 = jnp.float32
BF16 = jnp.bfloat16
LANES = 128
ROOM = 400 << 10
ROOM2 = 11200 << 10


def _nt(a, b):
    return lax.dot_general(a, b, (((1,), (1,)), ((), ())), preferred_element_type=F32)


def _iota(shape, dim):
    return lax.broadcasted_iota(jnp.int32, shape, dim)


def _parity_sign(common, bits):
    parity = jnp.zeros_like(common)
    for shift in range(bits):
        parity = parity ^ (lax.shift_right_logical(common, shift) & 1)
    return 1.0 - 2.0 * parity.astype(F32)


def _split(x):
    hi = x.astype(BF16)
    return hi, (x - hi.astype(F32)).astype(BF16)


def _butterfly(parts):
    parts = list(parts)
    step = 1
    while step < len(parts):
        for k in range(len(parts)):
            if not k & step:
                a, b = parts[k], parts[k + step]
                parts[k], parts[k + step] = a + b, a - b
        step *= 2
    return parts


def _sketch_kernel(
    samples, signs, target, matrix, keep, send, had, even, odd, held, sign_v, goal_v, mixed, got, turn, rhs, wide, spot, index, sems
):
    cols = matrix.shape[0]

    def fetch(i, q):
        at = pl.ds(pl.multiple_of(q * 16384 + i * 2048, 2048), 2048)
        return pltpu.make_async_copy(matrix.at[:, at], held.at[:, at], sems.at[i, q])

    first = pltpu.make_async_copy(samples, wide, sems.at[8, 2])
    first.start()
    small = [
        pltpu.make_async_copy(signs, sign_v, sems.at[8, 0]),
        pltpu.make_async_copy(target, goal_v, sems.at[8, 1]),
    ]
    for copy in small:
        copy.start()
    for i in range(8):
        for q in range(4):
            fetch(i, q).start()
    h = _parity_sign(_iota((128, 128), 0) & _iota((128, 128), 1), 7).astype(BF16)
    had[...] = jnp.concatenate([h, h], axis=1)
    me = lax.axis_index("row")
    first.wait()
    rows = wide[...]
    spot[...] = rows & 16383
    last = pltpu.make_async_copy(spot, index, sems.at[8, 3])
    last.start()
    common = lax.shift_right_logical(rows, 16) & me
    for q in range(4):
        group = lax.shift_right_logical(rows, 14) & q
        parity = _parity_sign(common, 6) * _parity_sign(group, 2)
        turn[q] = parity * (1.0 / 2048.0)
    rhs[...] = jnp.zeros_like(rhs)
    for copy in small:
        copy.wait()

    def spread(i, dest):
        totals = [rhs[c * 16 : c * 16 + 16, :] for c in range(cols // 16)]
        for q in range(4):
            row0 = pl.multiple_of(q * 128 + i * 16, 16)
            sign = sign_v[pl.ds(row0, 16), :].astype(F32)
            goal = goal_v[pl.ds(row0, 16), :]
            for c in range(cols // 16):
                parts = []
                for t in range(16):
                    at = pl.multiple_of(q * 16384 + i * 2048 + t * LANES, LANES)
                    x = held[c * 16 : c * 16 + 16, pl.ds(at, LANES)]
                    totals[c] = totals[c] + x * goal[t : t + 1, :]
                    parts.append(x * sign[t : t + 1, :])
                for t, y in enumerate(_butterfly(parts)):
                    hi, lo = _split(y)
                    at = (t & 1) * LANES + q * cols + c * 16
                    dest[t // 2, at : at + 16, :LANES] = hi
                    dest[t // 2, at : at + 16, LANES:] = lo
        for c in range(cols // 16):
            rhs[c * 16 : c * 16 + 16, :] = totals[c]

    def combine(i, source):
        for p in range(8):
            y = _nt(had[...], source[p])
            at = pl.multiple_of(i * 2048 + p * 256, 256)
            mixed[pl.ds(at, 128), :] = y[:, :LANES]
            mixed[pl.ds(at + 128, 128), :] = y[:, LANES:]

    @pl.loop(0, 4)
    def _(s):
        for k in range(2):
            for q in range(4):
                fetch(s * 2 + k, q).wait()
        combine(jnp.maximum(s * 2 - 1, 0), odd)
        spread(s * 2, even)
        combine(s * 2, even)
        spread(s * 2 + 1, odd)

    combine(7, odd)

    @pl.loop(0, 256, unroll=8)
    def _(r):
        at = [pl.ds(pl.multiple_of(i * 2048 + r * 8, 8), 8) for i in range(8)]
        for where, y in zip(at, _butterfly([mixed[where, :] for where in at])):
            mixed[where, :] = y

    core, x = me & 1, lax.shift_right_logical(me, 1 + 3)
    ones = jnp.ones((8, LANES), BF16)
    parts = []
    rest = rhs[...]
    for _i in range(3):
        piece = rest.astype(BF16)
        rest = rest - piece.astype(F32)
        parts.append(_nt(ones, piece))
    b_row = (parts[0] + parts[1]) + parts[2]
    b_row = jnp.concatenate([b_row] * (LANES // cols), axis=1)
    mine = _iota((8, LANES), 1) // cols == lax.axis_index("col")
    b_row = jnp.where(mine, b_row, 0.0)
    b_row = jnp.concatenate([b_row, jnp.zeros_like(b_row)], axis=1)
    eye = (_iota((LANES, LANES), 0) == _iota((LANES, LANES), 1)).astype(BF16)
    eye = jnp.concatenate([eye, eye], axis=1)

    last.wait()

    def source(chunk):
        return (core ^ lax.shift_right_logical(chunk, 2)) * 4 + ((x + chunk) & 3)

    @pl.loop(0, 16)
    def _(line):
        src = source(lax.shift_right_logical(line, 1)) * 2 + (line & 1)
        dest = pl.multiple_of(line * LANES, LANES)
        for k in range(LANES):
            got[pl.ds(dest + k, 1), :] = mixed[pl.ds(index[src, k], 1), :]

    for part, out in enumerate((keep, send)):

        @pl.loop(0, 4, unroll=2)
        def _(k, part=part, out=out):
            chunk = part * 4 + k
            group = source(chunk)
            hi, lo = _split(got[pl.ds(pl.multiple_of(chunk * 256, 256), 256), :])
            y = _nt(eye, jnp.concatenate([hi, lo], axis=1))
            total = None
            for q in range(4):
                sign = jnp.concatenate([turn[q, pl.ds(group * 2 + c, 1), :] for c in range(2)], axis=1)
                term = y[q * cols : (q + 1) * cols, :] * sign
                total = term if total is None else total + term
            out[k, :cols, :] = total
            out[k, cols:, :] = b_row


def _sketch(matrix, signs, target, samples):
    cols, rows = matrix.shape
    vmem = pl.BlockSpec(memory_space=pltpu.VMEM)
    hbm = pl.BlockSpec(memory_space=pltpu.HBM)
    return pl.pallas_call(
        _sketch_kernel,
        in_specs=[hbm] * 4,
        out_specs=[vmem] * 2,
        scratch_shapes=[
            pltpu.VMEM((LANES, 256), BF16),
            pltpu.VMEM((8, 256, 256), BF16),
            pltpu.VMEM((8, 256, 256), BF16),
            pltpu.VMEM((cols, rows), F32),
            pltpu.VMEM((512, LANES), jnp.int32),
            pltpu.VMEM((512, LANES), F32),
            pltpu.VMEM((16384, LANES), F32),
            pltpu.VMEM((2048, LANES), F32),
            pltpu.VMEM((4, 16, LANES), F32),
            pltpu.VMEM((cols, LANES), F32),
            pltpu.VMEM((16, LANES), jnp.int32),
            pltpu.VMEM((16, LANES), jnp.int32),
            pltpu.SMEM((16, LANES), jnp.int32),
            pltpu.SemaphoreType.DMA((9, 4)),
        ],
        out_shape=[jax.ShapeDtypeStruct((4, cols + 8, 256), F32)] * 2,
        compiler_params=pltpu.CompilerParams(vmem_limit_bytes=67043328 - ROOM),
        name="sketch",
    )(samples.reshape(16, LANES), signs.reshape(512, LANES), target.reshape(512, LANES), matrix)


def _gram_kernel(s0, s1, s2, s3, gram, b_row, whole):
    cols = s0.shape[0] - 8
    for k, s in enumerate((s0, s1, s2, s3)):
        at = lax.rem(lax.axis_index("col") + k, 4) * cols
        whole[pl.ds(pl.multiple_of(at, cols), cols), :] = s[:cols, :]
    s = whole[...]
    hi = s.astype(BF16)
    rest = s - hi.astype(F32)
    mid = rest.astype(BF16)
    lo = (rest - mid.astype(F32)).astype(BF16)
    cross = _nt(hi, mid)
    cross2 = _nt(hi, lo)
    small = (cross2 + cross2.T) + _nt(mid, mid)
    gram[...] = _nt(hi, hi) + ((cross + cross.T) + small)
    b_row[...] = (s0[cols:, :LANES] + s2[cols:, :LANES]) + (s1[cols:, :LANES] + s3[cols:, :LANES])


def _gram(pieces):
    vmem = pl.BlockSpec(memory_space=pltpu.VMEM)
    return pl.pallas_call(
        _gram_kernel,
        in_specs=[vmem] * 4,
        out_specs=[vmem] * 2,
        out_shape=[jax.ShapeDtypeStruct((128, 128), F32), jax.ShapeDtypeStruct((8, 128), F32)],
        scratch_shapes=[pltpu.VMEM((128, 256), F32)],
        compiler_params=pltpu.CompilerParams(vmem_limit_bytes=8 << 20),
        name="gram",
    )(*pieces)


def _eliminate(work, extra, lane, sub):
    work, extra = list(work), list(extra)
    count = len(work)
    for t in range(count):
        columns = {i: [work[i][:, 8 * t + j : 8 * t + j + 1] for j in range(8)] for i in range(t, count)}
        columns = {i: [jnp.broadcast_to(c, sub.shape) for c in v] for i, v in columns.items()}
        for r in range(8):
            pivot = [jnp.broadcast_to(c[r : r + 1, :], sub.shape) for c in columns[t]]
            inverse = 1.0 / pivot[r]
            row = jnp.broadcast_to(work[t][r : r + 1, :], sub.shape)
            row2 = jnp.broadcast_to(extra[t][r : r + 1, :], sub.shape)
            for i in range(t, count):
                factor = columns[i][r] * inverse
                if i == t:
                    factor = jnp.where(sub > r, factor, 0.0)
                for j in range(r + 1, 8):
                    columns[i][j] = columns[i][j] - factor * pivot[j]
                work[i] = work[i] - factor * row
                extra[i] = extra[i] - factor * row2
    pivots = [
        jnp.sum(jnp.where(lane == sub + 8 * t, work[t], 0.0), axis=1, keepdims=True) for t in range(count)
    ]
    return work, extra, pivots


def _rows_sum(parts):
    total = parts[0]
    for part in parts[1:]:
        total = total + part
    return jnp.sum(total, axis=0, keepdims=True)


def _fit_kernel(g0, g1, b_row, target, matrix, gradient, fitted, held, goal, sem):
    cols = matrix.shape[0]
    copies = [pltpu.make_async_copy(target, goal, sem.at[cols // 8])]
    copies += [
        pltpu.make_async_copy(matrix.at[8 * i : 8 * i + 8, :], held.at[8 * i : 8 * i + 8, :], sem.at[i])
        for i in range(cols // 8)
    ]
    for copy in copies:
        copy.start()
    n, h, half = 128, 64, 8
    lane, sub = _iota((8, n), 1), _iota((8, n), 0)
    left = lane < h
    tiles = [(g0[8 * t : 8 * t + 8, :] + g1[8 * t : 8 * t + 8, :]) * 2048.0 for t in range(16)]
    right = b_row[...]
    b = [jnp.sum(jnp.where(lane == sub + 8 * t, right[:1, :], 0.0), axis=1, keepdims=True) for t in range(16)]
    ident = [jnp.where(lane == sub + 8 * t + h, 1.0, 0.0) for t in range(half)]
    work = [jnp.where(left, tiles[t], ident[t]) for t in range(half)]
    extra = [jnp.where(left, pltpu.roll(tiles[t], h, 1), b[t]) for t in range(half)]
    w1, y1, d1 = _eliminate(work, extra, lane, sub)
    scaled = jnp.concatenate([y * (1.0 / d) for y, d in zip(y1, d1)], axis=0)
    product = lax.dot_general(
        scaled.T[:h, :],
        jnp.concatenate(y1, axis=0),
        (((1,), (0,)), ((), ())),
        precision=lax.Precision.HIGHEST,
        preferred_element_type=F32,
    )
    product = [product[8 * t : 8 * t + 8, :] for t in range(half)]
    work = [jnp.where(left, pltpu.roll(tiles[half + t], h, 1) - product[t], ident[t]) for t in range(half)]
    extra = [b[half + t] - product[t] for t in range(half)]
    w2, z2, d2 = _eliminate(work, extra, lane, sub)
    z2 = [z[:, h : h + 1] for z in z2]
    est2 = _rows_sum([w * (z / d) for w, z, d in zip(w2, z2, d2)])
    low2 = pltpu.roll(jnp.broadcast_to(est2, (8, n)), h, 1)
    z1 = [y[:, h : h + 1] for y in y1]
    rest = [z - jnp.sum(jnp.where(left, y * low2, 0.0), axis=1, keepdims=True) for z, y in zip(z1, y1)]
    est1 = _rows_sum([w * (z / d) for w, z, d in zip(w1, rest, d1)])
    est = jnp.where(left, pltpu.roll(jnp.broadcast_to(est1, (8, n)), h, 1), est2)
    gradient[...] = _rows_sum(
        [
            jnp.where(lane == sub + 8 * t, z * lax.rsqrt(d), 0.0)
            for t, (z, d) in enumerate(zip(z1 + z2, d1 + d2))
        ]
    )
    first = lax.axis_index("col") * cols
    e = [
        jnp.broadcast_to(
            jnp.sum(jnp.where(lane == sub + (first + 8 * i), -est, 0.0), axis=1, keepdims=True), (8, n)
        )
        for i in range(cols // 8)
    ]
    for copy in copies:
        copy.wait()

    weight = jnp.where(first == 0, 1.0, 0.0)

    def fold(u, v, step):
        low = (sub & step) == 0
        other = jnp.where(low, v, u)
        return jnp.where(low, u, v) + pltpu.roll(other, step, 0)

    @pl.loop(0, 64, unroll=4)
    def _(k8):
        rows = []
        for k in range(8):
            at = pl.multiple_of((k8 * 8 + k) * LANES, LANES)
            acc = None
            for i in range(cols // 8):
                term = held[8 * i : 8 * i + 8, pl.ds(at, LANES)] * e[i]
                acc = term if acc is None else acc + term
            rows.append(acc)
        for step in (1, 2, 4):
            rows = [fold(rows[k], rows[k + 1], step) for k in range(0, len(rows), 2)]
        at = pl.ds(pl.multiple_of(k8 * 8, 8), 8)
        fitted[at, :] = rows[0] + goal[at, :] * weight


def _fit(g0, g1, b_row, target, matrix):
    cols, rows = matrix.shape
    vmem = pl.BlockSpec(memory_space=pltpu.VMEM)
    return pl.pallas_call(
        _fit_kernel,
        in_specs=[vmem] * 3 + [pl.BlockSpec(memory_space=pltpu.HBM)] * 2,
        out_specs=[vmem] * 2,
        out_shape=[jax.ShapeDtypeStruct((1, 128), F32), jax.ShapeDtypeStruct((rows // LANES, LANES), F32)],
        scratch_shapes=[
            pltpu.VMEM((cols, rows), F32),
            pltpu.VMEM((rows // LANES, LANES), F32),
            pltpu.SemaphoreType.DMA((cols // 8 + 1,)),
        ],
        compiler_params=pltpu.CompilerParams(vmem_limit_bytes=67043328 - ROOM2),
        name="fit",
    )(g0, g1, b_row, target.reshape(rows // LANES, LANES), matrix)


def _row_pairs(dx=0, dz=0, dcore=0):
    pairs = []
    for i in range(64):
        x, z, core = i >> 4, (i >> 1) & 7, i & 1
        pairs.append((i, (((x + dx) % 4) << 4) | (((z + dz) % 8) << 1) | (core ^ dcore)))
    return pairs


def _ring(k):
    return [(i, (i + k) % 4) for i in range(4)]


def _sum4(own, others):
    return (own + others[1]) + (others[0] + others[2])


def body(matrix, row_signs, sample_rows, target):
    cols, rows = matrix.shape
    chunks, send = _sketch(matrix, row_signs, target, sample_rows)
    chunks = chunks + lax.ppermute(send, "row", _row_pairs(dcore=1))
    piece = _sum4(chunks[0], [lax.ppermute(chunks[k], "row", _row_pairs(dx=k)) for k in (1, 2, 3)])
    piece = piece + lax.ppermute(piece, "row", _row_pairs(dz=4))
    piece = _sum4(piece, [lax.ppermute(piece, "row", _row_pairs(dz=k)) for k in (1, 2, -1)])
    pieces = [piece] + [lax.ppermute(piece, "col", _ring(-k)) for k in (1, 2, 3)]
    gram, b_row = _gram(pieces)
    gram = gram + lax.ppermute(gram, "row", _row_pairs(dcore=1))
    turned = [lax.ppermute(gram, "row", _row_pairs(dx=k)) for k in (1, 2, 3)]
    gradient, rest = _fit(gram + turned[1], turned[0] + turned[2], b_row, target, matrix)
    rest = _sum4(rest, [lax.ppermute(rest, "col", _ring(k)) for k in (1, 2, 3)])
    return (gradient.reshape(128), rest.reshape(rows))


def solution(mesh):
    return jax.shard_map(
        body,
        mesh=mesh,
        in_specs=(P("col", "row"), P("row"), P(), P("row")),
        out_specs=(P(), P("row")),
        check_vma=False,
    )
```

```python
import jax
import jax.numpy as jnp
from jax import lax
from jax.experimental import pallas as pl
from jax.experimental.pallas import tpu as pltpu
from jax.sharding import PartitionSpec as P

F32 = jnp.float32
BF16 = jnp.bfloat16
LANES = 128
ROOM = 400 << 10
ROOM2 = 11200 << 10


def _nt(a, b):
    return lax.dot_general(a, b, (((1,), (1,)), ((), ())), preferred_element_type=F32)


def _iota(shape, dim):
    return lax.broadcasted_iota(jnp.int32, shape, dim)


def _parity_sign(common, bits):
    parity = jnp.zeros_like(common)
    for shift in range(bits):
        parity = parity ^ (lax.shift_right_logical(common, shift) & 1)
    return 1.0 - 2.0 * parity.astype(F32)


def _split(x):
    hi = x.astype(BF16)
    return hi, (x - hi.astype(F32)).astype(BF16)


def _butterfly(parts):
    parts = list(parts)
    step = 1
    while step < len(parts):
        for k in range(len(parts)):
            if not k & step:
                a, b = parts[k], parts[k + step]
                parts[k], parts[k + step] = a + b, a - b
        step *= 2
    return parts


def _sketch_kernel(
    samples, signs, target, matrix, keep, send, had, even, odd, held, sign_v, goal_v, mixed, got, turn, rhs, wide, spot, index, sems
):
    cols = matrix.shape[0]

    def fetch(i, q):
        at = pl.ds(pl.multiple_of(q * 16384 + i * 2048, 2048), 2048)
        return pltpu.make_async_copy(matrix.at[:, at], held.at[:, at], sems.at[i, q])

    first = pltpu.make_async_copy(samples, wide, sems.at[8, 2])
    first.start()
    small = [
        pltpu.make_async_copy(signs, sign_v, sems.at[8, 0]),
        pltpu.make_async_copy(target, goal_v, sems.at[8, 1]),
    ]
    for copy in small:
        copy.start()
    for i in range(8):
        for q in range(4):
            fetch(i, q).start()
    h = _parity_sign(_iota((128, 128), 0) & _iota((128, 128), 1), 7).astype(BF16)
    had[...] = jnp.concatenate([h, h], axis=1)
    me = lax.axis_index("row")
    first.wait()
    rows = wide[...]
    spot[...] = rows & 16383
    last = pltpu.make_async_copy(spot, index, sems.at[8, 3])
    last.start()
    common = lax.shift_right_logical(rows, 16) & me
    for q in range(4):
        group = lax.shift_right_logical(rows, 14) & q
        parity = _parity_sign(common, 6) * _parity_sign(group, 2)
        turn[q] = parity * (1.0 / 2048.0)
    rhs[...] = jnp.zeros_like(rhs)
    for copy in small:
        copy.wait()

    def spread(i, dest):
        totals = [rhs[c * 16 : c * 16 + 16, :] for c in range(cols // 16)]
        for q in range(4):
            row0 = pl.multiple_of(q * 128 + i * 16, 16)
            sign = sign_v[pl.ds(row0, 16), :].astype(F32)
            goal = goal_v[pl.ds(row0, 16), :]
            for c in range(cols // 16):
                parts = []
                for t in range(16):
                    at = pl.multiple_of(q * 16384 + i * 2048 + t * LANES, LANES)
                    x = held[c * 16 : c * 16 + 16, pl.ds(at, LANES)]
                    totals[c] = totals[c] + x * goal[t : t + 1, :]
                    parts.append(x * sign[t : t + 1, :])
                for t, y in enumerate(_butterfly(parts)):
                    hi, lo = _split(y)
                    at = (t & 1) * LANES + q * cols + c * 16
                    dest[t // 2, at : at + 16, :LANES] = hi
                    dest[t // 2, at : at + 16, LANES:] = lo
        for c in range(cols // 16):
            rhs[c * 16 : c * 16 + 16, :] = totals[c]

    def combine(i, source):
        for p in range(8):
            y = _nt(had[...], source[p])
            at = pl.multiple_of(i * 2048 + p * 256, 256)
            mixed[pl.ds(at, 128), :] = y[:, :LANES]
            mixed[pl.ds(at + 128, 128), :] = y[:, LANES:]

    @pl.loop(0, 4)
    def _(s):
        for k in range(2):
            for q in range(4):
                fetch(s * 2 + k, q).wait()
        combine(jnp.maximum(s * 2 - 1, 0), odd)
        spread(s * 2, even)
        combine(s * 2, even)
        spread(s * 2 + 1, odd)

    combine(7, odd)

    @pl.loop(0, 256, unroll=8)
    def _(r):
        at = [pl.ds(pl.multiple_of(i * 2048 + r * 8, 8), 8) for i in range(8)]
        for where, y in zip(at, _butterfly([mixed[where, :] for where in at])):
            mixed[where, :] = y

    core, x = me & 1, lax.shift_right_logical(me, 1 + 3)
    ones = jnp.ones((8, LANES), BF16)
    parts = []
    rest = rhs[...]
    for _i in range(3):
        piece = rest.astype(BF16)
        rest = rest - piece.astype(F32)
        parts.append(_nt(ones, piece))
    b_row = (parts[0] + parts[1]) + parts[2]
    b_row = jnp.concatenate([b_row] * (LANES // cols), axis=1)
    mine = _iota((8, LANES), 1) // cols == lax.axis_index("col")
    b_row = jnp.where(mine, b_row, 0.0)
    b_row = jnp.concatenate([b_row, jnp.zeros_like(b_row)], axis=1)
    eye = (_iota((LANES, LANES), 0) == _iota((LANES, LANES), 1)).astype(BF16)
    eye = jnp.concatenate([eye, eye], axis=1)

    last.wait()

    def source(chunk):
        return (core ^ lax.shift_right_logical(chunk, 2)) * 4 + ((x + chunk) & 3)

    @pl.loop(0, 16)
    def _(line):
        src = source(lax.shift_right_logical(line, 1)) * 2 + (line & 1)
        dest = pl.multiple_of(line * LANES, LANES)
        for k in range(LANES):
            got[pl.ds(dest + k, 1), :] = mixed[pl.ds(index[src, k], 1), :]

    for part, out in enumerate((keep, send)):

        @pl.loop(0, 4, unroll=2)
        def _(k, part=part, out=out):
            chunk = part * 4 + k
            group = source(chunk)
            hi, lo = _split(got[pl.ds(pl.multiple_of(chunk * 256, 256), 256), :])
            y = _nt(eye, jnp.concatenate([hi, lo], axis=1))
            total = None
            for q in range(4):
                sign = jnp.concatenate([turn[q, pl.ds(group * 2 + c, 1), :] for c in range(2)], axis=1)
                term = y[q * cols : (q + 1) * cols, :] * sign
                total = term if total is None else total + term
            out[k, :cols, :] = total
            out[k, cols:, :] = b_row


def _sketch(matrix, signs, target, samples):
    cols, rows = matrix.shape
    vmem = pl.BlockSpec(memory_space=pltpu.VMEM)
    hbm = pl.BlockSpec(memory_space=pltpu.HBM)
    return pl.pallas_call(
        _sketch_kernel,
        in_specs=[hbm] * 4,
        out_specs=[vmem] * 2,
        scratch_shapes=[
            pltpu.VMEM((LANES, 256), BF16),
            pltpu.VMEM((8, 256, 256), BF16),
            pltpu.VMEM((8, 256, 256), BF16),
            pltpu.VMEM((cols, rows), F32),
            pltpu.VMEM((512, LANES), jnp.int32),
            pltpu.VMEM((512, LANES), F32),
            pltpu.VMEM((16384, LANES), F32),
            pltpu.VMEM((2048, LANES), F32),
            pltpu.VMEM((4, 16, LANES), F32),
            pltpu.VMEM((cols, LANES), F32),
            pltpu.VMEM((16, LANES), jnp.int32),
            pltpu.VMEM((16, LANES), jnp.int32),
            pltpu.SMEM((16, LANES), jnp.int32),
            pltpu.SemaphoreType.DMA((9, 4)),
        ],
        out_shape=[jax.ShapeDtypeStruct((4, cols + 8, 256), F32)] * 2,
        compiler_params=pltpu.CompilerParams(vmem_limit_bytes=67043328 - ROOM),
        name="sketch",
    )(samples.reshape(16, LANES), signs.reshape(512, LANES), target.reshape(512, LANES), matrix)


def _gram_kernel(s0, s1, s2, s3, gram, b_row, whole):
    cols = s0.shape[0] - 8
    for k, s in enumerate((s0, s1, s2, s3)):
        at = lax.rem(lax.axis_index("col") + k, 4) * cols
        whole[pl.ds(pl.multiple_of(at, cols), cols), :] = s[:cols, :]
    s = whole[...]
    hi = s.astype(BF16)
    rest = s - hi.astype(F32)
    mid = rest.astype(BF16)
    lo = (rest - mid.astype(F32)).astype(BF16)
    cross = _nt(hi, mid)
    cross2 = _nt(hi, lo)
    small = (cross2 + cross2.T) + _nt(mid, mid)
    gram[...] = _nt(hi, hi) + ((cross + cross.T) + small)
    b_row[...] = (s0[cols:, :LANES] + s2[cols:, :LANES]) + (s1[cols:, :LANES] + s3[cols:, :LANES])


def _gram(pieces):
    vmem = pl.BlockSpec(memory_space=pltpu.VMEM)
    return pl.pallas_call(
        _gram_kernel,
        in_specs=[vmem] * 4,
        out_specs=[vmem] * 2,
        out_shape=[jax.ShapeDtypeStruct((128, 128), F32), jax.ShapeDtypeStruct((8, 128), F32)],
        scratch_shapes=[pltpu.VMEM((128, 256), F32)],
        compiler_params=pltpu.CompilerParams(vmem_limit_bytes=8 << 20),
        name="gram",
    )(*pieces)


def _eliminate(work, extra, lane, sub):
    work, extra = list(work), list(extra)
    count = len(work)
    for t in range(count):
        columns = {i: [work[i][:, 8 * t + j : 8 * t + j + 1] for j in range(8)] for i in range(t, count)}
        columns = {i: [jnp.broadcast_to(c, sub.shape) for c in v] for i, v in columns.items()}
        for r in range(8):
            pivot = [jnp.broadcast_to(c[r : r + 1, :], sub.shape) for c in columns[t]]
            inverse = 1.0 / pivot[r]
            row = jnp.broadcast_to(work[t][r : r + 1, :], sub.shape)
            row2 = jnp.broadcast_to(extra[t][r : r + 1, :], sub.shape)
            for i in range(t, count):
                factor = columns[i][r] * inverse
                if i == t:
                    factor = jnp.where(sub > r, factor, 0.0)
                for j in range(r + 1, 8):
                    columns[i][j] = columns[i][j] - factor * pivot[j]
                work[i] = work[i] - factor * row
                extra[i] = extra[i] - factor * row2
    pivots = [
        jnp.sum(jnp.where(lane == sub + 8 * t, work[t], 0.0), axis=1, keepdims=True) for t in range(count)
    ]
    return work, extra, pivots


def _rows_sum(parts):
    total = parts[0]
    for part in parts[1:]:
        total = total + part
    return jnp.sum(total, axis=0, keepdims=True)


def _fit_kernel(g0, g1, b_row, target, matrix, gradient, upper, lower, held, goal, sem):
    cols = matrix.shape[0]
    copies = [pltpu.make_async_copy(target, goal, sem.at[cols // 8])]
    copies += [
        pltpu.make_async_copy(matrix.at[8 * i : 8 * i + 8, :], held.at[8 * i : 8 * i + 8, :], sem.at[i])
        for i in range(cols // 8)
    ]
    for copy in copies:
        copy.start()
    n, h, half = 128, 64, 8
    lane, sub = _iota((8, n), 1), _iota((8, n), 0)
    left = lane < h
    tiles = [(g0[8 * t : 8 * t + 8, :] + g1[8 * t : 8 * t + 8, :]) * 2048.0 for t in range(16)]
    right = b_row[...]
    b = [jnp.sum(jnp.where(lane == sub + 8 * t, right[:1, :], 0.0), axis=1, keepdims=True) for t in range(16)]
    ident = [jnp.where(lane == sub + 8 * t + h, 1.0, 0.0) for t in range(half)]
    work = [jnp.where(left, tiles[t], ident[t]) for t in range(half)]
    extra = [jnp.where(left, pltpu.roll(tiles[t], h, 1), b[t]) for t in range(half)]
    w1, y1, d1 = _eliminate(work, extra, lane, sub)
    scaled = jnp.concatenate([y * (1.0 / d) for y, d in zip(y1, d1)], axis=0)
    product = lax.dot_general(
        scaled.T[:h, :],
        jnp.concatenate(y1, axis=0),
        (((1,), (0,)), ((), ())),
        precision=lax.Precision.HIGHEST,
        preferred_element_type=F32,
    )
    product = [product[8 * t : 8 * t + 8, :] for t in range(half)]
    work = [jnp.where(left, pltpu.roll(tiles[half + t], h, 1) - product[t], ident[t]) for t in range(half)]
    extra = [b[half + t] - product[t] for t in range(half)]
    w2, z2, d2 = _eliminate(work, extra, lane, sub)
    z2 = [z[:, h : h + 1] for z in z2]
    est2 = _rows_sum([w * (z / d) for w, z, d in zip(w2, z2, d2)])
    low2 = pltpu.roll(jnp.broadcast_to(est2, (8, n)), h, 1)
    z1 = [y[:, h : h + 1] for y in y1]
    rest = [z - jnp.sum(jnp.where(left, y * low2, 0.0), axis=1, keepdims=True) for z, y in zip(z1, y1)]
    est1 = _rows_sum([w * (z / d) for w, z, d in zip(w1, rest, d1)])
    est = jnp.where(left, pltpu.roll(jnp.broadcast_to(est1, (8, n)), h, 1), est2)
    gradient[...] = _rows_sum(
        [
            jnp.where(lane == sub + 8 * t, z * lax.rsqrt(d), 0.0)
            for t, (z, d) in enumerate(zip(z1 + z2, d1 + d2))
        ]
    )
    first = lax.axis_index("col") * cols
    e = [
        jnp.broadcast_to(
            jnp.sum(jnp.where(lane == sub + (first + 8 * i), -est, 0.0), axis=1, keepdims=True), (8, n)
        )
        for i in range(cols // 8)
    ]
    for copy in copies:
        copy.wait()

    weight = jnp.where(first == 0, 1.0, 0.0)

    def fold(u, v, step):
        low = (sub & step) == 0
        other = jnp.where(low, v, u)
        return jnp.where(low, u, v) + pltpu.roll(other, step, 0)

    for first_row, out in ((0, upper), (256, lower)):

        @pl.loop(0, 32, unroll=4)
        def _(k8, first_row=first_row, out=out):
            rows = []
            for k in range(8):
                at = pl.multiple_of((first_row + k8 * 8 + k) * LANES, LANES)
                acc = None
                for i in range(cols // 8):
                    term = held[8 * i : 8 * i + 8, pl.ds(at, LANES)] * e[i]
                    acc = term if acc is None else acc + term
                rows.append(acc)
            for step in (1, 2, 4):
                rows = [fold(rows[k], rows[k + 1], step) for k in range(0, len(rows), 2)]
            at = pl.multiple_of(k8 * 8, 8)
            share = goal[pl.ds(first_row + at, 8), :] * weight
            out[pl.ds(at, 8), :] = rows[0] + share


def _fit(g0, g1, b_row, target, matrix):
    cols, rows = matrix.shape
    vmem = pl.BlockSpec(memory_space=pltpu.VMEM)
    return pl.pallas_call(
        _fit_kernel,
        in_specs=[vmem] * 3 + [pl.BlockSpec(memory_space=pltpu.HBM)] * 2,
        out_specs=[vmem] * 3,
        out_shape=[jax.ShapeDtypeStruct((1, 128), F32)] + [jax.ShapeDtypeStruct((rows // LANES // 2, LANES), F32)] * 2,
        scratch_shapes=[
            pltpu.VMEM((cols, rows), F32),
            pltpu.VMEM((rows // LANES, LANES), F32),
            pltpu.SemaphoreType.DMA((cols // 8 + 1,)),
        ],
        compiler_params=pltpu.CompilerParams(vmem_limit_bytes=67043328 - ROOM2),
        name="fit",
    )(g0, g1, b_row, target.reshape(rows // LANES, LANES), matrix)


def _row_pairs(x_to=None, z_to=None, core_to=None):
    pairs = []
    for i in range(64):
        x, z, core = i >> 4, (i >> 1) & 7, i & 1
        x = x_to(x) if x_to else x
        z = z_to(z) if z_to else z
        core = core_to(core) if core_to else core
        pairs.append((i, (x << 4) | (z << 1) | core))
    return pairs


def _flip(k):
    return lambda i: i ^ k


def _turn(k, size):
    return lambda i: (i + k) % size


def _swap(value, **to):
    return lax.ppermute(value, "row", _row_pairs(**to))


def _col_swap(value, k):
    return lax.ppermute(value, "col", [(i, i ^ k) for i in range(4)])


def _sum_z(piece):
    near = piece + _swap(piece, z_to=_flip(1))
    next_to = _swap(near, z_to=lambda z: (z + 1) % 8 if z & 1 else (z - 1) % 8)
    far = _swap(jnp.stack([near, next_to]), z_to=lambda z: (z - 3) % 8 if z & 1 else (z + 3) % 8)
    z = (lax.axis_index("row") >> 1) & 3
    inner = (z == 1) | (z == 2)
    return (near + jnp.where(inner, next_to, far[0])) + (jnp.where(inner, far[0], next_to) + far[1])


def _ring(k):
    return [(i, (i + k) % 4) for i in range(4)]


def _sum4(own, others):
    return (own + others[1]) + (others[0] + others[2])


def body(matrix, row_signs, sample_rows, target):
    cols, rows = matrix.shape
    chunks, send = _sketch(matrix, row_signs, target, sample_rows)
    chunks = chunks + _swap(send, core_to=_flip(1))
    piece = _sum4(chunks[0], [_swap(chunks[k], x_to=_turn(k, 4)) for k in (1, 2, 3)])
    piece = _sum_z(piece)
    pieces = [piece] + [lax.ppermute(piece, "col", _ring(-k)) for k in (1, 2, 3)]
    gram, b_row = _gram(pieces)
    gram = gram + _swap(gram, core_to=_flip(1))
    gram = gram + _swap(gram, x_to=_flip(1))
    gradient, upper, lower = _fit(gram, _swap(gram, x_to=_flip(3)), b_row, target, matrix)
    upper, lower = upper + _col_swap(upper, 1), lower + _col_swap(lower, 3)
    upper, lower = upper + _col_swap(upper, 3), lower + _col_swap(lower, 1)
    return (gradient.reshape(128), jnp.concatenate([upper, lower]).reshape(rows))


def solution(mesh):
    return jax.shard_map(
        body,
        mesh=mesh,
        in_specs=(P("col", "row"), P("row"), P(), P("row")),
        out_specs=(P(), P("row")),
        check_vma=False,
    )
```

```python
import jax
import jax.numpy as jnp
from jax import lax
from jax.experimental import pallas as pl
from jax.experimental.pallas import tpu as pltpu
from jax.sharding import PartitionSpec as P

F32 = jnp.float32
BF16 = jnp.bfloat16
LANES = 128
ROOM = 400 << 10
ROOM2 = 11200 << 10


def _nt(a, b):
    return lax.dot_general(a, b, (((1,), (1,)), ((), ())), preferred_element_type=F32)


def _iota(shape, dim):
    return lax.broadcasted_iota(jnp.int32, shape, dim)


def _parity_sign(common, bits):
    parity = jnp.zeros_like(common)
    for shift in range(bits):
        parity = parity ^ (lax.shift_right_logical(common, shift) & 1)
    return 1.0 - 2.0 * parity.astype(F32)


def _split(x):
    hi = x.astype(BF16)
    return hi, (x - hi.astype(F32)).astype(BF16)


def _butterfly(parts):
    parts = list(parts)
    step = 1
    while step < len(parts):
        for k in range(len(parts)):
            if not k & step:
                a, b = parts[k], parts[k + step]
                parts[k], parts[k + step] = a + b, a - b
        step *= 2
    return parts


def _sketch_kernel(
    samples, signs, target, matrix, keep, send, had, even, odd, held, sign_v, goal_v, mixed, got, turn, rhs, wide, spot, index, sems
):
    cols = matrix.shape[0]

    def fetch(i, q):
        at = pl.ds(pl.multiple_of(q * 16384 + i * 2048, 2048), 2048)
        return pltpu.make_async_copy(matrix.at[:, at], held.at[:, at], sems.at[i, q])

    first = pltpu.make_async_copy(samples, wide, sems.at[8, 2])
    first.start()
    small = [
        pltpu.make_async_copy(signs, sign_v, sems.at[8, 0]),
        pltpu.make_async_copy(target, goal_v, sems.at[8, 1]),
    ]
    for copy in small:
        copy.start()
    for i in range(8):
        for q in range(4):
            fetch(i, q).start()
    h = _parity_sign(_iota((128, 128), 0) & _iota((128, 128), 1), 7).astype(BF16)
    had[...] = jnp.concatenate([h, h], axis=1)
    me = lax.axis_index("row")
    first.wait()
    rows = wide[...]
    spot[...] = rows & 16383
    last = pltpu.make_async_copy(spot, index, sems.at[8, 3])
    last.start()
    common = lax.shift_right_logical(rows, 16) & me
    for q in range(4):
        group = lax.shift_right_logical(rows, 14) & q
        parity = _parity_sign(common, 6) * _parity_sign(group, 2)
        turn[q] = parity * (1.0 / 2048.0)
    rhs[...] = jnp.zeros_like(rhs)
    for copy in small:
        copy.wait()

    def spread(i, dest):
        totals = [rhs[c * 16 : c * 16 + 16, :] for c in range(cols // 16)]
        for q in range(4):
            row0 = pl.multiple_of(q * 128 + i * 16, 16)
            sign = sign_v[pl.ds(row0, 16), :].astype(F32)
            goal = goal_v[pl.ds(row0, 16), :]
            for c in range(cols // 16):
                parts = []
                for t in range(16):
                    at = pl.multiple_of(q * 16384 + i * 2048 + t * LANES, LANES)
                    x = held[c * 16 : c * 16 + 16, pl.ds(at, LANES)]
                    totals[c] = totals[c] + x * goal[t : t + 1, :]
                    parts.append(x * sign[t : t + 1, :])
                for t, y in enumerate(_butterfly(parts)):
                    hi, lo = _split(y)
                    at = (t & 1) * LANES + q * cols + c * 16
                    dest[t // 2, at : at + 16, :LANES] = hi
                    dest[t // 2, at : at + 16, LANES:] = lo
        for c in range(cols // 16):
            rhs[c * 16 : c * 16 + 16, :] = totals[c]

    def combine(i, source):
        for p in range(8):
            y = _nt(had[...], source[p])
            at = pl.multiple_of(i * 2048 + p * 256, 256)
            mixed[pl.ds(at, 128), :] = y[:, :LANES]
            mixed[pl.ds(at + 128, 128), :] = y[:, LANES:]

    @pl.loop(0, 4)
    def _(s):
        for k in range(2):
            for q in range(4):
                fetch(s * 2 + k, q).wait()
        combine(jnp.maximum(s * 2 - 1, 0), odd)
        spread(s * 2, even)
        combine(s * 2, even)
        spread(s * 2 + 1, odd)

    combine(7, odd)

    @pl.loop(0, 256, unroll=8)
    def _(r):
        at = [pl.ds(pl.multiple_of(i * 2048 + r * 8, 8), 8) for i in range(8)]
        for where, y in zip(at, _butterfly([mixed[where, :] for where in at])):
            mixed[where, :] = y

    core, x = me & 1, lax.shift_right_logical(me, 1 + 3)
    ones = jnp.ones((8, LANES), BF16)
    parts = []
    rest = rhs[...]
    for _i in range(3):
        piece = rest.astype(BF16)
        rest = rest - piece.astype(F32)
        parts.append(_nt(ones, piece))
    b_row = (parts[0] + parts[1]) + parts[2]
    b_row = jnp.concatenate([b_row] * (LANES // cols), axis=1)
    mine = _iota((8, LANES), 1) // cols == lax.axis_index("col")
    b_row = jnp.where(mine, b_row, 0.0)
    b_row = jnp.concatenate([b_row, jnp.zeros_like(b_row)], axis=1)
    eye = (_iota((LANES, LANES), 0) == _iota((LANES, LANES), 1)).astype(BF16)
    eye = jnp.concatenate([eye, eye], axis=1)

    last.wait()

    def source(chunk):
        return (core ^ lax.shift_right_logical(chunk, 2)) * 4 + ((x + chunk) & 3)

    @pl.loop(0, 16)
    def _(line):
        src = source(lax.shift_right_logical(line, 1)) * 2 + (line & 1)
        dest = pl.multiple_of(line * LANES, LANES)
        for k in range(LANES):
            got[pl.ds(dest + k, 1), :] = mixed[pl.ds(index[src, k], 1), :]

    for part, out in enumerate((keep, send)):

        @pl.loop(0, 4, unroll=2)
        def _(k, part=part, out=out):
            chunk = part * 4 + k
            group = source(chunk)
            hi, lo = _split(got[pl.ds(pl.multiple_of(chunk * 256, 256), 256), :])
            y = _nt(eye, jnp.concatenate([hi, lo], axis=1))
            total = None
            for q in range(4):
                sign = jnp.concatenate([turn[q, pl.ds(group * 2 + c, 1), :] for c in range(2)], axis=1)
                term = y[q * cols : (q + 1) * cols, :] * sign
                total = term if total is None else total + term
            out[k, :cols, :] = total
            out[k, cols:, :] = b_row


def _sketch(matrix, signs, target, samples):
    cols, rows = matrix.shape
    vmem = pl.BlockSpec(memory_space=pltpu.VMEM)
    hbm = pl.BlockSpec(memory_space=pltpu.HBM)
    return pl.pallas_call(
        _sketch_kernel,
        in_specs=[hbm] * 4,
        out_specs=[vmem] * 2,
        scratch_shapes=[
            pltpu.VMEM((LANES, 256), BF16),
            pltpu.VMEM((8, 256, 256), BF16),
            pltpu.VMEM((8, 256, 256), BF16),
            pltpu.VMEM((cols, rows), F32),
            pltpu.VMEM((512, LANES), jnp.int32),
            pltpu.VMEM((512, LANES), F32),
            pltpu.VMEM((16384, LANES), F32),
            pltpu.VMEM((2048, LANES), F32),
            pltpu.VMEM((4, 16, LANES), F32),
            pltpu.VMEM((cols, LANES), F32),
            pltpu.VMEM((16, LANES), jnp.int32),
            pltpu.VMEM((16, LANES), jnp.int32),
            pltpu.SMEM((16, LANES), jnp.int32),
            pltpu.SemaphoreType.DMA((9, 4)),
        ],
        out_shape=[jax.ShapeDtypeStruct((4, cols + 8, 256), F32)] * 2,
        compiler_params=pltpu.CompilerParams(vmem_limit_bytes=67043328 - ROOM),
        name="sketch",
    )(samples.reshape(16, LANES), signs.reshape(512, LANES), target.reshape(512, LANES), matrix)


def _gram_kernel(s0, s1, s2, s3, gram, b_row, whole):
    cols = s0.shape[0] - 8
    for k, s in enumerate((s0, s1, s2, s3)):
        at = lax.rem(lax.axis_index("col") + k, 4) * cols
        whole[pl.ds(pl.multiple_of(at, cols), cols), :] = s[:cols, :]
    s = whole[...]
    hi = s.astype(BF16)
    rest = s - hi.astype(F32)
    mid = rest.astype(BF16)
    lo = (rest - mid.astype(F32)).astype(BF16)
    cross = _nt(hi, mid)
    cross2 = _nt(hi, lo)
    small = (cross2 + cross2.T) + _nt(mid, mid)
    gram[...] = _nt(hi, hi) + ((cross + cross.T) + small)
    b_row[...] = (s0[cols:, :LANES] + s2[cols:, :LANES]) + (s1[cols:, :LANES] + s3[cols:, :LANES])


def _gram(pieces):
    vmem = pl.BlockSpec(memory_space=pltpu.VMEM)
    return pl.pallas_call(
        _gram_kernel,
        in_specs=[vmem] * 4,
        out_specs=[vmem] * 2,
        out_shape=[jax.ShapeDtypeStruct((128, 128), F32), jax.ShapeDtypeStruct((8, 128), F32)],
        scratch_shapes=[pltpu.VMEM((128, 256), F32)],
        compiler_params=pltpu.CompilerParams(vmem_limit_bytes=8 << 20),
        name="gram",
    )(*pieces)


def _eliminate(work, extra, lane, sub):
    count = work.shape[0] // 8

    @pl.loop(0, count)
    def _(t):
        own = pl.ds(pl.multiple_of(t * 8, 8), 8)
        turn = lax.rem(128 - t * 8, 128)

        def columns_of(tile):
            tile = pltpu.roll(tile, turn, 1)
            return [jnp.broadcast_to(tile[:, j : j + 1], sub.shape) for j in range(8)]

        lead, lead2 = work[own, :], extra[own, :]
        head = columns_of(lead)
        pivot, inverse, row, row2 = [], [], [], []
        for r in range(8):
            spread = [jnp.broadcast_to(c[r : r + 1, :], sub.shape) for c in head]
            pivot.append(spread)
            inverse.append(1.0 / spread[r])
            row.append(jnp.broadcast_to(lead[r : r + 1, :], sub.shape))
            row2.append(jnp.broadcast_to(lead2[r : r + 1, :], sub.shape))
            factor = jnp.where(sub > r, head[r] * inverse[r], 0.0)
            for j in range(r + 1, 8):
                head[j] = head[j] - factor * spread[j]
            lead = lead - factor * row[r]
            lead2 = lead2 - factor * row2[r]
        for i in range(count):
            rows = slice(8 * i, 8 * i + 8)
            tile, tile2 = work[rows, :], extra[rows, :]
            below = jnp.where(i > t, 1.0, 0.0)
            columns = columns_of(tile)
            for r in range(8):
                factor = columns[r] * (inverse[r] * below)
                for j in range(r + 1, 8):
                    columns[j] = columns[j] - factor * pivot[r][j]
                tile = tile - factor * row[r]
                tile2 = tile2 - factor * row2[r]
            work[rows, :] = tile
            extra[rows, :] = tile2
        work[own, :] = lead
        extra[own, :] = lead2

    work = [work[8 * t : 8 * t + 8, :] for t in range(count)]
    extra = [extra[8 * t : 8 * t + 8, :] for t in range(count)]
    pivots = [
        jnp.sum(jnp.where(lane == sub + 8 * t, work[t], 0.0), axis=1, keepdims=True) for t in range(count)
    ]
    return work, extra, pivots


def _rows_sum(parts):
    total = parts[0]
    for part in parts[1:]:
        total = total + part
    return jnp.sum(total, axis=0, keepdims=True)


def _fit_kernel(g0, g1, b_row, target, matrix, gradient, upper, lower, held, goal, work_v, extra_v, sem):
    cols = matrix.shape[0]
    copies = [pltpu.make_async_copy(target, goal, sem.at[cols // 8])]
    copies += [
        pltpu.make_async_copy(matrix.at[8 * i : 8 * i + 8, :], held.at[8 * i : 8 * i + 8, :], sem.at[i])
        for i in range(cols // 8)
    ]
    for copy in copies:
        copy.start()
    n, h, half = 128, 64, 8
    lane, sub = _iota((8, n), 1), _iota((8, n), 0)
    left = lane < h
    tiles = [(g0[8 * t : 8 * t + 8, :] + g1[8 * t : 8 * t + 8, :]) * 2048.0 for t in range(16)]
    right = b_row[...]
    b = [jnp.sum(jnp.where(lane == sub + 8 * t, right[:1, :], 0.0), axis=1, keepdims=True) for t in range(16)]
    ident = [jnp.where(lane == sub + 8 * t + h, 1.0, 0.0) for t in range(half)]
    work = [jnp.where(left, tiles[t], ident[t]) for t in range(half)]
    extra = [jnp.where(left, pltpu.roll(tiles[t], h, 1), b[t]) for t in range(half)]
    work_v[...] = jnp.concatenate(work, axis=0)
    extra_v[...] = jnp.concatenate(extra, axis=0)
    w1, y1, d1 = _eliminate(work_v, extra_v, lane, sub)
    scaled = jnp.concatenate([y * (1.0 / d) for y, d in zip(y1, d1)], axis=0)
    product = lax.dot_general(
        scaled.T[:h, :],
        jnp.concatenate(y1, axis=0),
        (((1,), (0,)), ((), ())),
        precision=lax.Precision.HIGHEST,
        preferred_element_type=F32,
    )
    product = [product[8 * t : 8 * t + 8, :] for t in range(half)]
    work = [jnp.where(left, pltpu.roll(tiles[half + t], h, 1) - product[t], ident[t]) for t in range(half)]
    extra = [b[half + t] - product[t] for t in range(half)]
    work_v[...] = jnp.concatenate(work, axis=0)
    extra_v[...] = jnp.concatenate([jnp.broadcast_to(x, (8, n)) for x in extra], axis=0)
    w2, z2, d2 = _eliminate(work_v, extra_v, lane, sub)
    z2 = [z[:, h : h + 1] for z in z2]
    est2 = _rows_sum([w * (z / d) for w, z, d in zip(w2, z2, d2)])
    low2 = pltpu.roll(jnp.broadcast_to(est2, (8, n)), h, 1)
    z1 = [y[:, h : h + 1] for y in y1]
    rest = [z - jnp.sum(jnp.where(left, y * low2, 0.0), axis=1, keepdims=True) for z, y in zip(z1, y1)]
    est1 = _rows_sum([w * (z / d) for w, z, d in zip(w1, rest, d1)])
    est = jnp.where(left, pltpu.roll(jnp.broadcast_to(est1, (8, n)), h, 1), est2)
    gradient[...] = _rows_sum(
        [
            jnp.where(lane == sub + 8 * t, z * lax.rsqrt(d), 0.0)
            for t, (z, d) in enumerate(zip(z1 + z2, d1 + d2))
        ]
    )
    first = lax.axis_index("col") * cols
    e = [
        jnp.broadcast_to(
            jnp.sum(jnp.where(lane == sub + (first + 8 * i), -est, 0.0), axis=1, keepdims=True), (8, n)
        )
        for i in range(cols // 8)
    ]
    for copy in copies:
        copy.wait()

    weight = jnp.where(first == 0, 1.0, 0.0)

    def fold(u, v, step):
        low = (sub & step) == 0
        other = jnp.where(low, v, u)
        return jnp.where(low, u, v) + pltpu.roll(other, step, 0)

    for first_row, out in ((0, upper), (256, lower)):

        @pl.loop(0, 32, unroll=4)
        def _(k8, first_row=first_row, out=out):
            rows = []
            for k in range(8):
                at = pl.multiple_of((first_row + k8 * 8 + k) * LANES, LANES)
                acc = None
                for i in range(cols // 8):
                    term = held[8 * i : 8 * i + 8, pl.ds(at, LANES)] * e[i]
                    acc = term if acc is None else acc + term
                rows.append(acc)
            for step in (1, 2, 4):
                rows = [fold(rows[k], rows[k + 1], step) for k in range(0, len(rows), 2)]
            at = pl.multiple_of(k8 * 8, 8)
            share = goal[pl.ds(first_row + at, 8), :] * weight
            out[pl.ds(at, 8), :] = rows[0] + share


def _fit(g0, g1, b_row, target, matrix):
    cols, rows = matrix.shape
    vmem = pl.BlockSpec(memory_space=pltpu.VMEM)
    return pl.pallas_call(
        _fit_kernel,
        in_specs=[vmem] * 3 + [pl.BlockSpec(memory_space=pltpu.HBM)] * 2,
        out_specs=[vmem] * 3,
        out_shape=[jax.ShapeDtypeStruct((1, 128), F32)] + [jax.ShapeDtypeStruct((rows // LANES // 2, LANES), F32)] * 2,
        scratch_shapes=[
            pltpu.VMEM((cols, rows), F32),
            pltpu.VMEM((rows // LANES, LANES), F32),
            pltpu.VMEM((64, 128), F32),
            pltpu.VMEM((64, 128), F32),
            pltpu.SemaphoreType.DMA((cols // 8 + 1,)),
        ],
        compiler_params=pltpu.CompilerParams(vmem_limit_bytes=67043328 - ROOM2),
        name="fit",
    )(g0, g1, b_row, target.reshape(rows // LANES, LANES), matrix)


def _row_pairs(x_to=None, z_to=None, core_to=None):
    pairs = []
    for i in range(64):
        x, z, core = i >> 4, (i >> 1) & 7, i & 1
        x = x_to(x) if x_to else x
        z = z_to(z) if z_to else z
        core = core_to(core) if core_to else core
        pairs.append((i, (x << 4) | (z << 1) | core))
    return pairs


def _flip(k):
    return lambda i: i ^ k


def _turn(k, size):
    return lambda i: (i + k) % size


def _swap(value, **to):
    return lax.ppermute(value, "row", _row_pairs(**to))


def _col_swap(value, k):
    return lax.ppermute(value, "col", [(i, i ^ k) for i in range(4)])


def _sum_z(piece):
    groups = [[(x << 4) | (z << 1) | core for z in range(8)] for x in range(4) for core in range(2)]
    sent = jnp.broadcast_to(piece, (8,) + piece.shape)
    parts = lax.all_to_all(sent, "row", 0, 0, axis_index_groups=groups, tiled=True)
    pairs = [parts[k] + parts[k + 1] for k in range(0, 8, 2)]
    return (pairs[0] + pairs[1]) + (pairs[2] + pairs[3])


def _ring(k):
    return [(i, (i + k) % 4) for i in range(4)]


def _sum4(own, others):
    return (own + others[1]) + (others[0] + others[2])


def body(matrix, row_signs, sample_rows, target):
    cols, rows = matrix.shape
    chunks, send = _sketch(matrix, row_signs, target, sample_rows)
    chunks = chunks + _swap(send, core_to=_flip(1))
    piece = _sum4(chunks[0], [_swap(chunks[k], x_to=_turn(k, 4)) for k in (1, 2, 3)])
    piece = _sum_z(piece)
    pieces = [piece] + [lax.ppermute(piece, "col", _ring(-k)) for k in (1, 2, 3)]
    gram, b_row = _gram(pieces)
    gram = gram + _swap(gram, core_to=_flip(1))
    gram = gram + _swap(gram, x_to=_flip(1))
    gradient, upper, lower = _fit(gram, _swap(gram, x_to=_flip(3)), b_row, target, matrix)
    upper, lower = upper + _col_swap(upper, 1), lower + _col_swap(lower, 3)
    upper, lower = upper + _col_swap(upper, 3), lower + _col_swap(lower, 1)
    return (gradient.reshape(128), jnp.concatenate([upper, lower]).reshape(rows))


def solution(mesh):
    return jax.shard_map(
        body,
        mesh=mesh,
        in_specs=(P("col", "row"), P("row"), P(), P("row")),
        out_specs=(P(), P("row")),
        check_vma=False,
    )
```

```python
import jax
import jax.numpy as jnp
from jax import lax
from jax.experimental import pallas as pl
from jax.experimental.pallas import tpu as pltpu
from jax.sharding import PartitionSpec as P

F32 = jnp.float32
BF16 = jnp.bfloat16
LANES = 128
ROOM = 400 << 10
ROOM2 = 11200 << 10


def _nt(a, b):
    return lax.dot_general(a, b, (((1,), (1,)), ((), ())), preferred_element_type=F32)


def _iota(shape, dim):
    return lax.broadcasted_iota(jnp.int32, shape, dim)


def _parity_sign(common, bits):
    parity = jnp.zeros_like(common)
    for shift in range(bits):
        parity = parity ^ (lax.shift_right_logical(common, shift) & 1)
    return 1.0 - 2.0 * parity.astype(F32)


def _split(x):
    hi = x.astype(BF16)
    return hi, (x - hi.astype(F32)).astype(BF16)


def _butterfly(parts):
    parts = list(parts)
    step = 1
    while step < len(parts):
        for k in range(len(parts)):
            if not k & step:
                a, b = parts[k], parts[k + step]
                parts[k], parts[k + step] = a + b, a - b
        step *= 2
    return parts


def _sketch_kernel(
    samples, signs, target, matrix, keep, send, had, even, odd, held, sign_v, goal_v, mixed, got, turn, rhs, wide, spot, index, sems
):
    cols = matrix.shape[0]

    def fetch(i, q):
        at = pl.ds(pl.multiple_of(q * 16384 + i * 2048, 2048), 2048)
        return pltpu.make_async_copy(matrix.at[:, at], held.at[:, at], sems.at[i, q])

    first = pltpu.make_async_copy(samples, wide, sems.at[8, 2])
    first.start()
    small = [
        pltpu.make_async_copy(signs, sign_v, sems.at[8, 0]),
        pltpu.make_async_copy(target, goal_v, sems.at[8, 1]),
    ]
    for copy in small:
        copy.start()
    for i in range(8):
        for q in range(4):
            fetch(i, q).start()
    h = _parity_sign(_iota((128, 128), 0) & _iota((128, 128), 1), 7).astype(BF16)
    had[...] = jnp.concatenate([h, h], axis=1)
    me = lax.axis_index("row")
    first.wait()
    rows = wide[...]
    spot[...] = rows & 16383
    last = pltpu.make_async_copy(spot, index, sems.at[8, 3])
    last.start()
    common = lax.shift_right_logical(rows, 16) & me
    for q in range(4):
        group = lax.shift_right_logical(rows, 14) & q
        parity = _parity_sign(common, 6) * _parity_sign(group, 2)
        turn[q] = parity * (1.0 / 2048.0)
    rhs[...] = jnp.zeros_like(rhs)
    for copy in small:
        copy.wait()

    def spread(i, dest):
        totals = [rhs[c * 16 : c * 16 + 16, :] for c in range(cols // 16)]
        for q in range(4):
            row0 = pl.multiple_of(q * 128 + i * 16, 16)
            sign = sign_v[pl.ds(row0, 16), :].astype(F32)
            goal = goal_v[pl.ds(row0, 16), :]
            for c in range(cols // 16):
                parts = []
                for t in range(16):
                    at = pl.multiple_of(q * 16384 + i * 2048 + t * LANES, LANES)
                    x = held[c * 16 : c * 16 + 16, pl.ds(at, LANES)]
                    totals[c] = totals[c] + x * goal[t : t + 1, :]
                    parts.append(x * sign[t : t + 1, :])
                for t, y in enumerate(_butterfly(parts)):
                    hi, lo = _split(y)
                    at = (t & 1) * LANES + q * cols + c * 16
                    dest[t // 2, at : at + 16, :LANES] = hi
                    dest[t // 2, at : at + 16, LANES:] = lo
        for c in range(cols // 16):
            rhs[c * 16 : c * 16 + 16, :] = totals[c]

    def combine(i, source):
        for p in range(8):
            y = _nt(had[...], source[p])
            at = pl.multiple_of(i * 2048 + p * 256, 256)
            mixed[pl.ds(at, 128), :] = y[:, :LANES]
            mixed[pl.ds(at + 128, 128), :] = y[:, LANES:]

    @pl.loop(0, 4)
    def _(s):
        for q in range(4):
            fetch(s * 2, q).wait()
        combine(jnp.maximum(s * 2 - 1, 0), odd)
        spread(s * 2, even)
        for q in range(4):
            fetch(s * 2 + 1, q).wait()
        combine(s * 2, even)
        spread(s * 2 + 1, odd)

    combine(7, odd)

    @pl.loop(0, 256, unroll=8)
    def _(r):
        at = [pl.ds(pl.multiple_of(i * 2048 + r * 8, 8), 8) for i in range(8)]
        for where, y in zip(at, _butterfly([mixed[where, :] for where in at])):
            mixed[where, :] = y

    core, x = me & 1, lax.shift_right_logical(me, 1 + 3)
    ones = jnp.ones((8, LANES), BF16)
    parts = []
    rest = rhs[...]
    for _i in range(3):
        piece = rest.astype(BF16)
        rest = rest - piece.astype(F32)
        parts.append(_nt(ones, piece))
    b_row = (parts[0] + parts[1]) + parts[2]
    b_row = jnp.concatenate([b_row] * (LANES // cols), axis=1)
    mine = _iota((8, LANES), 1) // cols == lax.axis_index("col")
    b_row = jnp.where(mine, b_row, 0.0)
    b_row = jnp.concatenate([b_row, jnp.zeros_like(b_row)], axis=1)
    eye = (_iota((LANES, LANES), 0) == _iota((LANES, LANES), 1)).astype(BF16)
    eye = jnp.concatenate([eye, eye], axis=1)

    last.wait()

    def source(chunk):
        return (core ^ lax.shift_right_logical(chunk, 2)) * 4 + ((x + chunk) & 3)

    @pl.loop(0, 16)
    def _(line):
        src = source(lax.shift_right_logical(line, 1)) * 2 + (line & 1)
        dest = pl.multiple_of(line * LANES, LANES)
        for k in range(LANES):
            got[pl.ds(dest + k, 1), :] = mixed[pl.ds(index[src, k], 1), :]

    for part, out in enumerate((keep, send)):

        @pl.loop(0, 4, unroll=2)
        def _(k, part=part, out=out):
            chunk = part * 4 + k
            group = source(chunk)
            hi, lo = _split(got[pl.ds(pl.multiple_of(chunk * 256, 256), 256), :])
            y = _nt(eye, jnp.concatenate([hi, lo], axis=1))
            total = None
            for q in range(4):
                sign = jnp.concatenate([turn[q, pl.ds(group * 2 + c, 1), :] for c in range(2)], axis=1)
                term = y[q * cols : (q + 1) * cols, :] * sign
                total = term if total is None else total + term
            out[k, :cols, :] = total
            out[k, cols:, :] = b_row


def _sketch(matrix, signs, target, samples):
    cols, rows = matrix.shape
    vmem = pl.BlockSpec(memory_space=pltpu.VMEM)
    hbm = pl.BlockSpec(memory_space=pltpu.HBM)
    return pl.pallas_call(
        _sketch_kernel,
        in_specs=[hbm] * 4,
        out_specs=[vmem] * 2,
        scratch_shapes=[
            pltpu.VMEM((LANES, 256), BF16),
            pltpu.VMEM((8, 256, 256), BF16),
            pltpu.VMEM((8, 256, 256), BF16),
            pltpu.VMEM((cols, rows), F32),
            pltpu.VMEM((512, LANES), jnp.int32),
            pltpu.VMEM((512, LANES), F32),
            pltpu.VMEM((16384, LANES), F32),
            pltpu.VMEM((2048, LANES), F32),
            pltpu.VMEM((4, 16, LANES), F32),
            pltpu.VMEM((cols, LANES), F32),
            pltpu.VMEM((16, LANES), jnp.int32),
            pltpu.VMEM((16, LANES), jnp.int32),
            pltpu.SMEM((16, LANES), jnp.int32),
            pltpu.SemaphoreType.DMA((9, 4)),
        ],
        out_shape=[jax.ShapeDtypeStruct((4, cols + 8, 256), F32)] * 2,
        compiler_params=pltpu.CompilerParams(vmem_limit_bytes=67043328 - ROOM),
        name="sketch",
    )(samples.reshape(16, LANES), signs.reshape(512, LANES), target.reshape(512, LANES), matrix)


def _gram_kernel(s0, s1, s2, s3, gram, b_row, whole):
    cols = s0.shape[0] - 8
    for k, s in enumerate((s0, s1, s2, s3)):
        at = lax.rem(lax.axis_index("col") + k, 4) * cols
        whole[pl.ds(pl.multiple_of(at, cols), cols), :] = s[:cols, :]
    s = whole[...]
    hi = s.astype(BF16)
    rest = s - hi.astype(F32)
    mid = rest.astype(BF16)
    lo = (rest - mid.astype(F32)).astype(BF16)
    cross = _nt(hi, mid)
    cross2 = _nt(hi, lo)
    small = (cross2 + cross2.T) + _nt(mid, mid)
    gram[...] = _nt(hi, hi) + ((cross + cross.T) + small)
    b_row[...] = (s0[cols:, :LANES] + s2[cols:, :LANES]) + (s1[cols:, :LANES] + s3[cols:, :LANES])


def _gram(pieces):
    vmem = pl.BlockSpec(memory_space=pltpu.VMEM)
    return pl.pallas_call(
        _gram_kernel,
        in_specs=[vmem] * 4,
        out_specs=[vmem] * 2,
        out_shape=[jax.ShapeDtypeStruct((128, 128), F32), jax.ShapeDtypeStruct((8, 128), F32)],
        scratch_shapes=[pltpu.VMEM((128, 256), F32)],
        compiler_params=pltpu.CompilerParams(vmem_limit_bytes=8 << 20),
        name="gram",
    )(*pieces)


def _eliminate(work, extra, lane, sub):
    count = work.shape[0] // 8

    @pl.loop(0, count)
    def _(t):
        own = pl.ds(pl.multiple_of(t * 8, 8), 8)
        turn = lax.rem(128 - t * 8, 128)

        def columns_of(tile):
            tile = pltpu.roll(tile, turn, 1)
            return [jnp.broadcast_to(tile[:, j : j + 1], sub.shape) for j in range(8)]

        lead, lead2 = work[own, :], extra[own, :]
        head = columns_of(lead)
        pivot, inverse, row, row2 = [], [], [], []
        for r in range(8):
            spread = [jnp.broadcast_to(c[r : r + 1, :], sub.shape) for c in head]
            pivot.append(spread)
            inverse.append(1.0 / spread[r])
            row.append(jnp.broadcast_to(lead[r : r + 1, :], sub.shape))
            row2.append(jnp.broadcast_to(lead2[r : r + 1, :], sub.shape))
            factor = jnp.where(sub > r, head[r] * inverse[r], 0.0)
            for j in range(r + 1, 8):
                head[j] = head[j] - factor * spread[j]
            lead = lead - factor * row[r]
            lead2 = lead2 - factor * row2[r]
        for i in range(count):
            rows = slice(8 * i, 8 * i + 8)
            tile, tile2 = work[rows, :], extra[rows, :]
            below = jnp.where(i > t, 1.0, 0.0)
            columns = columns_of(tile)
            for r in range(8):
                factor = columns[r] * (inverse[r] * below)
                for j in range(r + 1, 8):
                    columns[j] = columns[j] - factor * pivot[r][j]
                tile = tile - factor * row[r]
                tile2 = tile2 - factor * row2[r]
            work[rows, :] = tile
            extra[rows, :] = tile2
        work[own, :] = lead
        extra[own, :] = lead2

    work = [work[8 * t : 8 * t + 8, :] for t in range(count)]
    extra = [extra[8 * t : 8 * t + 8, :] for t in range(count)]
    pivots = [
        jnp.sum(jnp.where(lane == sub + 8 * t, work[t], 0.0), axis=1, keepdims=True) for t in range(count)
    ]
    return work, extra, pivots


def _rows_sum(parts):
    total = parts[0]
    for part in parts[1:]:
        total = total + part
    return jnp.sum(total, axis=0, keepdims=True)


def _fit_kernel(g0, g1, g2, g3, b_row, target, matrix, gradient, upper, lower, held, goal, work_v, extra_v, sem):
    cols = matrix.shape[0]
    copies = [pltpu.make_async_copy(target, goal, sem.at[cols // 8])]
    copies += [
        pltpu.make_async_copy(matrix.at[8 * i : 8 * i + 8, :], held.at[8 * i : 8 * i + 8, :], sem.at[i])
        for i in range(cols // 8)
    ]
    for copy in copies:
        copy.start()
    n, h, half = 128, 64, 8
    lane, sub = _iota((8, n), 1), _iota((8, n), 0)
    left = lane < h
    tiles = []
    for t in range(16):
        rows = slice(8 * t, 8 * t + 8)
        tiles.append(((g0[rows, :] + g2[rows, :]) + (g1[rows, :] + g3[rows, :])) * 2048.0)
    right = b_row[...]
    b = [jnp.sum(jnp.where(lane == sub + 8 * t, right[:1, :], 0.0), axis=1, keepdims=True) for t in range(16)]
    ident = [jnp.where(lane == sub + 8 * t + h, 1.0, 0.0) for t in range(half)]
    work = [jnp.where(left, tiles[t], ident[t]) for t in range(half)]
    extra = [jnp.where(left, pltpu.roll(tiles[t], h, 1), b[t]) for t in range(half)]
    work_v[...] = jnp.concatenate(work, axis=0)
    extra_v[...] = jnp.concatenate(extra, axis=0)
    w1, y1, d1 = _eliminate(work_v, extra_v, lane, sub)
    scaled = jnp.concatenate([y * (1.0 / d) for y, d in zip(y1, d1)], axis=0)
    product = lax.dot_general(
        scaled.T[:h, :],
        jnp.concatenate(y1, axis=0),
        (((1,), (0,)), ((), ())),
        precision=lax.Precision.HIGHEST,
        preferred_element_type=F32,
    )
    product = [product[8 * t : 8 * t + 8, :] for t in range(half)]
    work = [jnp.where(left, pltpu.roll(tiles[half + t], h, 1) - product[t], ident[t]) for t in range(half)]
    extra = [b[half + t] - product[t] for t in range(half)]
    work_v[...] = jnp.concatenate(work, axis=0)
    extra_v[...] = jnp.concatenate([jnp.broadcast_to(x, (8, n)) for x in extra], axis=0)
    w2, z2, d2 = _eliminate(work_v, extra_v, lane, sub)
    z2 = [z[:, h : h + 1] for z in z2]
    est2 = _rows_sum([w * (z / d) for w, z, d in zip(w2, z2, d2)])
    low2 = pltpu.roll(jnp.broadcast_to(est2, (8, n)), h, 1)
    z1 = [y[:, h : h + 1] for y in y1]
    rest = [z - jnp.sum(jnp.where(left, y * low2, 0.0), axis=1, keepdims=True) for z, y in zip(z1, y1)]
    est1 = _rows_sum([w * (z / d) for w, z, d in zip(w1, rest, d1)])
    est = jnp.where(left, pltpu.roll(jnp.broadcast_to(est1, (8, n)), h, 1), est2)
    gradient[...] = _rows_sum(
        [
            jnp.where(lane == sub + 8 * t, z * lax.rsqrt(d), 0.0)
            for t, (z, d) in enumerate(zip(z1 + z2, d1 + d2))
        ]
    )
    first = lax.axis_index("col") * cols
    e = [
        jnp.broadcast_to(
            jnp.sum(jnp.where(lane == sub + (first + 8 * i), -est, 0.0), axis=1, keepdims=True), (8, n)
        )
        for i in range(cols // 8)
    ]
    for copy in copies:
        copy.wait()

    weight = jnp.where(first == 0, 1.0, 0.0)

    def fold(u, v, step):
        low = (sub & step) == 0
        other = jnp.where(low, v, u)
        return jnp.where(low, u, v) + pltpu.roll(other, step, 0)

    for first_row, out in ((0, upper), (256, lower)):

        @pl.loop(0, 32, unroll=4)
        def _(k8, first_row=first_row, out=out):
            rows = []
            for k in range(8):
                at = pl.multiple_of((first_row + k8 * 8 + k) * LANES, LANES)
                acc = None
                for i in range(cols // 8):
                    term = held[8 * i : 8 * i + 8, pl.ds(at, LANES)] * e[i]
                    acc = term if acc is None else acc + term
                rows.append(acc)
            for step in (1, 2, 4):
                rows = [fold(rows[k], rows[k + 1], step) for k in range(0, len(rows), 2)]
            at = pl.multiple_of(k8 * 8, 8)
            share = goal[pl.ds(first_row + at, 8), :] * weight
            out[pl.ds(at, 8), :] = rows[0] + share


def _fit(gram, others, b_row, target, matrix):
    cols, rows = matrix.shape
    vmem = pl.BlockSpec(memory_space=pltpu.VMEM)
    return pl.pallas_call(
        _fit_kernel,
        in_specs=[vmem] * 5 + [pl.BlockSpec(memory_space=pltpu.HBM)] * 2,
        out_specs=[vmem] * 3,
        out_shape=[jax.ShapeDtypeStruct((1, 128), F32)] + [jax.ShapeDtypeStruct((rows // LANES // 2, LANES), F32)] * 2,
        scratch_shapes=[
            pltpu.VMEM((cols, rows), F32),
            pltpu.VMEM((rows // LANES, LANES), F32),
            pltpu.VMEM((64, 128), F32),
            pltpu.VMEM((64, 128), F32),
            pltpu.SemaphoreType.DMA((cols // 8 + 1,)),
        ],
        compiler_params=pltpu.CompilerParams(vmem_limit_bytes=67043328 - ROOM2),
        name="fit",
    )(gram, *others, b_row, target.reshape(rows // LANES, LANES), matrix)


def _row_pairs(x_to=None, z_to=None, core_to=None):
    pairs = []
    for i in range(64):
        x, z, core = i >> 4, (i >> 1) & 7, i & 1
        x = x_to(x) if x_to else x
        z = z_to(z) if z_to else z
        core = core_to(core) if core_to else core
        pairs.append((i, (x << 4) | (z << 1) | core))
    return pairs


def _flip(k):
    return lambda i: i ^ k


def _turn(k, size):
    return lambda i: (i + k) % size


def _swap(value, **to):
    return lax.ppermute(value, "row", _row_pairs(**to))


def _col_swap(value, k):
    return lax.ppermute(value, "col", [(i, i ^ k) for i in range(4)])


def _ring(k):
    return [(i, (i + k) % 4) for i in range(4)]


def _sum4(own, others):
    return (own + others[1]) + (others[0] + others[2])


def body(matrix, row_signs, sample_rows, target):
    cols, rows = matrix.shape
    chunks, send = _sketch(matrix, row_signs, target, sample_rows)
    chunks = chunks + _swap(send, core_to=_flip(1))
    piece = _sum4(chunks[0], [_swap(chunks[k], x_to=_turn(k, 4)) for k in (1, 2, 3)])
    for bit in (1, 2, 4):
        piece = piece + _swap(piece, z_to=_flip(bit))
    pieces = [piece] + [lax.ppermute(piece, "col", _ring(-k)) for k in (1, 2, 3)]
    gram, b_row = _gram(pieces)
    gram = gram + _swap(gram, core_to=_flip(1))
    grams = [_swap(gram, x_to=_turn(k, 4)) for k in (1, 2, 3)]
    gradient, upper, lower = _fit(gram, grams, b_row, target, matrix)
    upper, lower = upper + _col_swap(upper, 1), lower + _col_swap(lower, 3)
    upper, lower = upper + _col_swap(upper, 3), lower + _col_swap(lower, 1)
    return (gradient.reshape(128), jnp.concatenate([upper, lower]).reshape(rows))


def solution(mesh):
    return jax.shard_map(
        body,
        mesh=mesh,
        in_specs=(P("col", "row"), P("row"), P(), P("row")),
        out_specs=(P(), P("row")),
        check_vma=False,
    )
```

```python
import jax
import jax.numpy as jnp
from jax import lax
from jax.experimental import pallas as pl
from jax.experimental.pallas import tpu as pltpu
from jax.sharding import PartitionSpec as P

F32 = jnp.float32
BF16 = jnp.bfloat16
LANES = 128
ROOM = 400 << 10
ROOM2 = 11200 << 10


def _nt(a, b):
    return lax.dot_general(a, b, (((1,), (1,)), ((), ())), preferred_element_type=F32)


def _iota(shape, dim):
    return lax.broadcasted_iota(jnp.int32, shape, dim)


def _parity_sign(common, bits):
    parity = jnp.zeros_like(common)
    for shift in range(bits):
        parity = parity ^ (lax.shift_right_logical(common, shift) & 1)
    return 1.0 - 2.0 * parity.astype(F32)


def _split(x):
    hi = x.astype(BF16)
    return hi, (x - hi.astype(F32)).astype(BF16)


def _butterfly(parts):
    parts = list(parts)
    step = 1
    while step < len(parts):
        for k in range(len(parts)):
            if not k & step:
                a, b = parts[k], parts[k + step]
                parts[k], parts[k + step] = a + b, a - b
        step *= 2
    return parts


def _sketch_kernel(
    samples, signs, target, matrix, keep, send, keep_v, send_v, had, even, odd, held, sign_v, goal_v, mixed, got, turn, rhs, wide, spot, index, sems
):
    cols = matrix.shape[0]

    def fetch(i, q):
        at = pl.ds(pl.multiple_of(q * 16384 + i * 2048, 2048), 2048)
        return pltpu.make_async_copy(matrix.at[:, at], held.at[:, at], sems.at[i, q])

    first = pltpu.make_async_copy(samples, wide, sems.at[8, 2])
    first.start()
    small = [
        pltpu.make_async_copy(signs, sign_v, sems.at[8, 0]),
        pltpu.make_async_copy(target, goal_v, sems.at[8, 1]),
    ]
    for copy in small:
        copy.start()
    for i in range(8):
        for q in range(4):
            fetch(i, q).start()
    h = _parity_sign(_iota((128, 128), 0) & _iota((128, 128), 1), 7).astype(BF16)
    had[...] = jnp.concatenate([h, h], axis=1)
    me = lax.axis_index("row")
    first.wait()
    rows = wide[...]
    spot[...] = rows & 16383
    last = pltpu.make_async_copy(spot, index, sems.at[8, 3])
    last.start()
    common = lax.shift_right_logical(rows, 16) & me
    for q in range(4):
        group = lax.shift_right_logical(rows, 14) & q
        parity = _parity_sign(common, 6) * _parity_sign(group, 2)
        turn[q] = parity * (1.0 / 2048.0)
    rhs[...] = jnp.zeros_like(rhs)
    for copy in small:
        copy.wait()

    def spread(i, dest):
        totals = [rhs[c * 16 : c * 16 + 16, :] for c in range(cols // 16)]
        for q in range(4):
            row0 = pl.multiple_of(q * 128 + i * 16, 16)
            sign = sign_v[pl.ds(row0, 16), :].astype(F32)
            goal = goal_v[pl.ds(row0, 16), :]
            for c in range(cols // 16):
                parts = []
                for t in range(16):
                    at = pl.multiple_of(q * 16384 + i * 2048 + t * LANES, LANES)
                    x = held[c * 16 : c * 16 + 16, pl.ds(at, LANES)]
                    totals[c] = totals[c] + x * goal[t : t + 1, :]
                    parts.append(x * sign[t : t + 1, :])
                for t, y in enumerate(_butterfly(parts)):
                    hi, lo = _split(y)
                    at = (t & 1) * LANES + q * cols + c * 16
                    dest[t // 2, at : at + 16, :LANES] = hi
                    dest[t // 2, at : at + 16, LANES:] = lo
        for c in range(cols // 16):
            rhs[c * 16 : c * 16 + 16, :] = totals[c]

    def combine(i, source):
        for p in range(8):
            y = _nt(had[...], source[p])
            at = pl.multiple_of(i * 2048 + p * 256, 256)
            mixed[pl.ds(at, 128), :] = y[:, :LANES]
            mixed[pl.ds(at + 128, 128), :] = y[:, LANES:]

    @pl.loop(0, 4)
    def _(s):
        for q in range(4):
            fetch(s * 2, q).wait()
        combine(jnp.maximum(s * 2 - 1, 0), odd)
        spread(s * 2, even)
        for q in range(4):
            fetch(s * 2 + 1, q).wait()
        combine(s * 2, even)
        spread(s * 2 + 1, odd)

    combine(7, odd)

    @pl.loop(0, 256, unroll=8)
    def _(r):
        at = [pl.ds(pl.multiple_of(i * 2048 + r * 8, 8), 8) for i in range(8)]
        for where, y in zip(at, _butterfly([mixed[where, :] for where in at])):
            mixed[where, :] = y

    core, x = me & 1, lax.shift_right_logical(me, 1 + 3)
    ones = jnp.ones((8, LANES), BF16)
    parts = []
    rest = rhs[...]
    for _i in range(3):
        piece = rest.astype(BF16)
        rest = rest - piece.astype(F32)
        parts.append(_nt(ones, piece))
    b_row = (parts[0] + parts[1]) + parts[2]
    b_row = jnp.concatenate([b_row] * (LANES // cols), axis=1)
    mine = _iota((8, LANES), 1) // cols == lax.axis_index("col")
    b_row = jnp.where(mine, b_row, 0.0)
    b_row = jnp.concatenate([b_row, jnp.zeros_like(b_row)], axis=1)
    eye = (_iota((LANES, LANES), 0) == _iota((LANES, LANES), 1)).astype(BF16)
    eye = jnp.concatenate([eye, eye], axis=1)

    last.wait()

    def source(chunk):
        return (core ^ lax.shift_right_logical(chunk, 2)) * 4 + ((x + chunk) & 3)

    @pl.loop(0, 16)
    def _(line):
        src = source(lax.shift_right_logical(line, 1)) * 2 + (line & 1)
        dest = pl.multiple_of(line * LANES, LANES)
        for k in range(LANES):
            got[pl.ds(dest + k, 1), :] = mixed[pl.ds(index[src, k], 1), :]

    leaving = []
    for part, out, final in ((1, send_v, send), (0, keep_v, keep)):

        @pl.loop(0, 4, unroll=2)
        def _(k, part=part, out=out):
            chunk = part * 4 + k
            group = source(chunk)
            hi, lo = _split(got[pl.ds(pl.multiple_of(chunk * 256, 256), 256), :])
            y = _nt(eye, jnp.concatenate([hi, lo], axis=1))
            total = None
            for q in range(4):
                sign = jnp.concatenate([turn[q, pl.ds(group * 2 + c, 1), :] for c in range(2)], axis=1)
                term = y[q * cols : (q + 1) * cols, :] * sign
                total = term if total is None else total + term
            out[k, :cols, :] = total
            out[k, cols:, :] = b_row

        leaving.append(pltpu.make_async_copy(out, final, sems.at[9, part]))
        leaving[-1].start()

    for copy in leaving:
        copy.wait()


def _sketch(matrix, signs, target, samples):
    cols, rows = matrix.shape
    hbm = pl.BlockSpec(memory_space=pltpu.HBM)
    return pl.pallas_call(
        _sketch_kernel,
        in_specs=[hbm] * 4,
        out_specs=[hbm] * 2,
        scratch_shapes=[
            pltpu.VMEM((4, cols + 8, 256), F32),
            pltpu.VMEM((4, cols + 8, 256), F32),
            pltpu.VMEM((LANES, 256), BF16),
            pltpu.VMEM((8, 256, 256), BF16),
            pltpu.VMEM((8, 256, 256), BF16),
            pltpu.VMEM((cols, rows), F32),
            pltpu.VMEM((512, LANES), jnp.int32),
            pltpu.VMEM((512, LANES), F32),
            pltpu.VMEM((16384, LANES), F32),
            pltpu.VMEM((2048, LANES), F32),
            pltpu.VMEM((4, 16, LANES), F32),
            pltpu.VMEM((cols, LANES), F32),
            pltpu.VMEM((16, LANES), jnp.int32),
            pltpu.VMEM((16, LANES), jnp.int32),
            pltpu.SMEM((16, LANES), jnp.int32),
            pltpu.SemaphoreType.DMA((10, 4)),
        ],
        out_shape=[jax.ShapeDtypeStruct((4, cols + 8, 256), F32)] * 2,
        compiler_params=pltpu.CompilerParams(vmem_limit_bytes=67043328 - ROOM),
        name="sketch",
    )(samples.reshape(16, LANES), signs.reshape(512, LANES), target.reshape(512, LANES), matrix)


def _gram_kernel(s0, s1, s2, s3, gram, b_row, whole):
    cols = s0.shape[0] - 8
    for k, s in enumerate((s0, s1, s2, s3)):
        at = lax.rem(lax.axis_index("col") + k, 4) * cols
        whole[pl.ds(pl.multiple_of(at, cols), cols), :] = s[:cols, :]
    s = whole[...]
    hi = s.astype(BF16)
    rest = s - hi.astype(F32)
    mid = rest.astype(BF16)
    lo = (rest - mid.astype(F32)).astype(BF16)
    cross = _nt(hi, mid)
    cross2 = _nt(hi, lo)
    small = (cross2 + cross2.T) + _nt(mid, mid)
    gram[...] = _nt(hi, hi) + ((cross + cross.T) + small)
    b_row[...] = (s0[cols:, :LANES] + s2[cols:, :LANES]) + (s1[cols:, :LANES] + s3[cols:, :LANES])


def _gram(pieces):
    vmem = pl.BlockSpec(memory_space=pltpu.VMEM)
    return pl.pallas_call(
        _gram_kernel,
        in_specs=[vmem] * 4,
        out_specs=[vmem] * 2,
        out_shape=[jax.ShapeDtypeStruct((128, 128), F32), jax.ShapeDtypeStruct((8, 128), F32)],
        scratch_shapes=[pltpu.VMEM((128, 256), F32)],
        compiler_params=pltpu.CompilerParams(vmem_limit_bytes=8 << 20),
        name="gram",
    )(*pieces)


def _eliminate(work, extra, lane, sub):
    count = work.shape[0] // 8

    @pl.loop(0, count)
    def _(t):
        own = pl.ds(pl.multiple_of(t * 8, 8), 8)
        turn = lax.rem(128 - t * 8, 128)

        def columns_of(tile):
            tile = pltpu.roll(tile, turn, 1)
            return [jnp.broadcast_to(tile[:, j : j + 1], sub.shape) for j in range(8)]

        lead, lead2 = work[own, :], extra[own, :]
        head = columns_of(lead)
        pivot, inverse, row, row2 = [], [], [], []
        for r in range(8):
            spread = [jnp.broadcast_to(c[r : r + 1, :], sub.shape) for c in head]
            pivot.append(spread)
            inverse.append(1.0 / spread[r])
            row.append(jnp.broadcast_to(lead[r : r + 1, :], sub.shape))
            row2.append(jnp.broadcast_to(lead2[r : r + 1, :], sub.shape))
            factor = jnp.where(sub > r, head[r] * inverse[r], 0.0)
            for j in range(r + 1, 8):
                head[j] = head[j] - factor * spread[j]
            lead = lead - factor * row[r]
            lead2 = lead2 - factor * row2[r]
        for i in range(count):
            rows = slice(8 * i, 8 * i + 8)
            tile, tile2 = work[rows, :], extra[rows, :]
            below = jnp.where(i > t, 1.0, 0.0)
            columns = columns_of(tile)
            for r in range(8):
                factor = columns[r] * (inverse[r] * below)
                for j in range(r + 1, 8):
                    columns[j] = columns[j] - factor * pivot[r][j]
                tile = tile - factor * row[r]
                tile2 = tile2 - factor * row2[r]
            work[rows, :] = tile
            extra[rows, :] = tile2
        work[own, :] = lead
        extra[own, :] = lead2

    work = [work[8 * t : 8 * t + 8, :] for t in range(count)]
    extra = [extra[8 * t : 8 * t + 8, :] for t in range(count)]
    pivots = [
        jnp.sum(jnp.where(lane == sub + 8 * t, work[t], 0.0), axis=1, keepdims=True) for t in range(count)
    ]
    return work, extra, pivots


def _rows_sum(parts):
    total = parts[0]
    for part in parts[1:]:
        total = total + part
    return jnp.sum(total, axis=0, keepdims=True)


def _fit_kernel(g0, g1, g2, g3, b_row, target, matrix, gradient, upper, lower, held, goal, work_v, extra_v, grad_v, sem):
    cols = matrix.shape[0]
    copies = [pltpu.make_async_copy(target, goal, sem.at[cols // 8])]
    copies += [
        pltpu.make_async_copy(matrix.at[8 * i : 8 * i + 8, :], held.at[8 * i : 8 * i + 8, :], sem.at[i])
        for i in range(cols // 8)
    ]
    for copy in copies:
        copy.start()
    n, h, half = 128, 64, 8
    lane, sub = _iota((8, n), 1), _iota((8, n), 0)
    left = lane < h
    tiles = []
    for t in range(16):
        rows = slice(8 * t, 8 * t + 8)
        tiles.append(((g0[rows, :] + g2[rows, :]) + (g1[rows, :] + g3[rows, :])) * 2048.0)
    right = b_row[...]
    b = [jnp.sum(jnp.where(lane == sub + 8 * t, right[:1, :], 0.0), axis=1, keepdims=True) for t in range(16)]
    ident = [jnp.where(lane == sub + 8 * t + h, 1.0, 0.0) for t in range(half)]
    work = [jnp.where(left, tiles[t], ident[t]) for t in range(half)]
    extra = [jnp.where(left, pltpu.roll(tiles[t], h, 1), b[t]) for t in range(half)]
    work_v[...] = jnp.concatenate(work, axis=0)
    extra_v[...] = jnp.concatenate(extra, axis=0)
    w1, y1, d1 = _eliminate(work_v, extra_v, lane, sub)
    scaled = jnp.concatenate([y * (1.0 / d) for y, d in zip(y1, d1)], axis=0)
    product = lax.dot_general(
        scaled.T[:h, :],
        jnp.concatenate(y1, axis=0),
        (((1,), (0,)), ((), ())),
        precision=lax.Precision.HIGHEST,
        preferred_element_type=F32,
    )
    product = [product[8 * t : 8 * t + 8, :] for t in range(half)]
    work = [jnp.where(left, pltpu.roll(tiles[half + t], h, 1) - product[t], ident[t]) for t in range(half)]
    extra = [b[half + t] - product[t] for t in range(half)]
    work_v[...] = jnp.concatenate(work, axis=0)
    extra_v[...] = jnp.concatenate([jnp.broadcast_to(x, (8, n)) for x in extra], axis=0)
    w2, z2, d2 = _eliminate(work_v, extra_v, lane, sub)
    z2 = [z[:, h : h + 1] for z in z2]
    est2 = _rows_sum([w * (z / d) for w, z, d in zip(w2, z2, d2)])
    low2 = pltpu.roll(jnp.broadcast_to(est2, (8, n)), h, 1)
    z1 = [y[:, h : h + 1] for y in y1]
    rest = [z - jnp.sum(jnp.where(left, y * low2, 0.0), axis=1, keepdims=True) for z, y in zip(z1, y1)]
    est1 = _rows_sum([w * (z / d) for w, z, d in zip(w1, rest, d1)])
    est = jnp.where(left, pltpu.roll(jnp.broadcast_to(est1, (8, n)), h, 1), est2)
    grad_v[...] = _rows_sum(
        [
            jnp.where(lane == sub + 8 * t, z * lax.rsqrt(d), 0.0)
            for t, (z, d) in enumerate(zip(z1 + z2, d1 + d2))
        ]
    )
    leaving = pltpu.make_async_copy(grad_v, gradient, sem.at[cols // 8 + 1])
    leaving.start()
    first = lax.axis_index("col") * cols
    e = [
        jnp.broadcast_to(
            jnp.sum(jnp.where(lane == sub + (first + 8 * i), -est, 0.0), axis=1, keepdims=True), (8, n)
        )
        for i in range(cols // 8)
    ]
    for copy in copies:
        copy.wait()

    weight = jnp.where(first == 0, 1.0, 0.0)

    def fold(u, v, step):
        low = (sub & step) == 0
        other = jnp.where(low, v, u)
        return jnp.where(low, u, v) + pltpu.roll(other, step, 0)

    for first_row, out in ((0, upper), (256, lower)):

        @pl.loop(0, 32, unroll=4)
        def _(k8, first_row=first_row, out=out):
            rows = []
            for k in range(8):
                at = pl.multiple_of((first_row + k8 * 8 + k) * LANES, LANES)
                acc = None
                for i in range(cols // 8):
                    term = held[8 * i : 8 * i + 8, pl.ds(at, LANES)] * e[i]
                    acc = term if acc is None else acc + term
                rows.append(acc)
            for step in (1, 2, 4):
                rows = [fold(rows[k], rows[k + 1], step) for k in range(0, len(rows), 2)]
            at = pl.multiple_of(k8 * 8, 8)
            share = goal[pl.ds(first_row + at, 8), :] * weight
            out[pl.ds(at, 8), :] = rows[0] + share

    leaving.wait()


def _fit(gram, others, b_row, target, matrix):
    cols, rows = matrix.shape
    vmem = pl.BlockSpec(memory_space=pltpu.VMEM)
    return pl.pallas_call(
        _fit_kernel,
        in_specs=[vmem] * 5 + [pl.BlockSpec(memory_space=pltpu.HBM)] * 2,
        out_specs=[pl.BlockSpec(memory_space=pltpu.HBM)] + [vmem] * 2,
        out_shape=[jax.ShapeDtypeStruct((1, 128), F32)] + [jax.ShapeDtypeStruct((rows // LANES // 2, LANES), F32)] * 2,
        scratch_shapes=[
            pltpu.VMEM((cols, rows), F32),
            pltpu.VMEM((rows // LANES, LANES), F32),
            pltpu.VMEM((64, 128), F32),
            pltpu.VMEM((64, 128), F32),
            pltpu.VMEM((1, 128), F32),
            pltpu.SemaphoreType.DMA((cols // 8 + 2,)),
        ],
        compiler_params=pltpu.CompilerParams(vmem_limit_bytes=67043328 - ROOM2),
        name="fit",
    )(gram, *others, b_row, target.reshape(rows // LANES, LANES), matrix)


def _row_pairs(x_to=None, z_to=None, core_to=None):
    pairs = []
    for i in range(64):
        x, z, core = i >> 4, (i >> 1) & 7, i & 1
        x = x_to(x) if x_to else x
        z = z_to(z) if z_to else z
        core = core_to(core) if core_to else core
        pairs.append((i, (x << 4) | (z << 1) | core))
    return pairs


def _flip(k):
    return lambda i: i ^ k


def _turn(k, size):
    return lambda i: (i + k) % size


def _swap(value, **to):
    return lax.ppermute(value, "row", _row_pairs(**to))


def _col_swap(value, k):
    return lax.ppermute(value, "col", [(i, i ^ k) for i in range(4)])


def _ring(k):
    return [(i, (i + k) % 4) for i in range(4)]


def _sum4(own, others):
    return (own + others[1]) + (others[0] + others[2])


def body(matrix, row_signs, sample_rows, target):
    cols, rows = matrix.shape
    chunks, send = _sketch(matrix, row_signs, target, sample_rows)
    chunks = chunks + _swap(send, core_to=_flip(1))
    piece = _sum4(chunks[0], [_swap(chunks[k], x_to=_turn(k, 4)) for k in (1, 2, 3)])
    for bit in (1, 2, 4):
        piece = piece + _swap(piece, z_to=_flip(bit))
    pieces = [piece] + [lax.ppermute(piece, "col", _ring(-k)) for k in (1, 2, 3)]
    gram, b_row = _gram(pieces)
    gram = gram + _swap(gram, core_to=_flip(1))
    grams = [_swap(gram, x_to=_turn(k, 4)) for k in (1, 2, 3)]
    gradient, upper, lower = _fit(gram, grams, b_row, target, matrix)
    upper, lower = upper + _col_swap(upper, 1), lower + _col_swap(lower, 3)
    upper, lower = upper + _col_swap(upper, 3), lower + _col_swap(lower, 1)
    return (gradient.reshape(128), jnp.concatenate([upper, lower]).reshape(rows))


def solution(mesh):
    return jax.shard_map(
        body,
        mesh=mesh,
        in_specs=(P("col", "row"), P("row"), P(), P("row")),
        out_specs=(P(), P("row")),
        check_vma=False,
    )
```
